256 devices in a mesh: dp: 4 (over x), tensor: 64 (over y, z, core).
Axes of the slice: x: 4, y: 4, z: 8, core: 2. Of those that a mesh axis runs over, the one named last changes fastest.
Arguments:
- tokens_in: bfloat16 [512, 4096], P('dp', 'tensor'), may hold values from -6 to 6
- out_grad: bfloat16 [512, 4096], P('dp', 'tensor'), may hold values from -6 to 6
- gate_blocks: bfloat16 [2048, 128, 128], P('tensor'), may hold values from -0.125 to 0.125
- up_blocks: bfloat16 [2048, 128, 128], P('tensor'), may hold values from -0.125 to 0.125
- down_blocks: bfloat16 [2048, 128, 128], P('tensor'), may hold values from -0.0625 to 0.0625
- gate_up_index: int32 [64, 32, 2], replicated, may hold values from 0 to 127, as said below
- down_index: int32 [64, 32, 2], replicated, may hold values from 0 to 127, as said below
Outputs:
- output: bfloat16 [512, 4096], P('dp', 'tensor')
- in_grad: bfloat16 [512, 4096], P('dp', 'tensor')
- gate_grads: bfloat16 [2048, 128, 128], P('tensor', 'dp')
- up_grads: bfloat16 [2048, 128, 128], P('tensor', 'dp')
- down_grads: bfloat16 [2048, 128, 128], P('tensor', 'dp')
The draws below stay inside these ranges and needn't reach their ends.
Inputs may be any that keep to these rules, and one draw needn't show every extreme that they name: `gate_up_index`: Model-width blocks lie in 0 to 31, hidden-unit blocks in 0 to 127. No block is listed twice. The owner of hidden-unit block j is index j // 2 of tensor. Of one index's 32 entries at most 1 name hidden-unit blocks of any one owner, and in every draw some owner has exactly 1 entries from every index; other owners get from none up to all indices. `down_index`: Hidden-unit blocks lie in 0 to 127, model-width blocks in 0 to 31. No block is listed twice. The owner of hidden-unit block j is index j // 2 of tensor. Of one index's 32 entries at most 1 name hidden-unit blocks of any one owner, and in every draw some owner has exactly 1 entries from every index; other owners get from none up to all indices.
All inputs are finite; a program needn't handle non-finite values.
Results may differ from the reference program's by a relative error of at most 0.022.
Values may be sent and summed in bfloat16 or wider, within the bound.
A program may use at most 128 MiB of HBM per device.

```python
import jax
import jax.numpy as jnp
from jax import lax

D = 4096
FF = 16384
BS = 128
TOK_DEV = 128
DB = 32
FB = 128
OWN = 2
CAP = 1
NNZ_DEV = 32
BLOCKS = 2048
TOKENS = 512
N_DP = 4
N_TENSOR = 64


def block_layout(key, which):
    last_owner = N_TENSOR - 1
    mat_key = jax.random.fold_in(key, which)
    pair_count = N_TENSOR // 2
    pair_sizes = jax.random.randint(jax.random.fold_in(mat_key, 1), (pair_count,), N_TENSOR // 4, N_TENSOR - N_TENSOR // 4 + 1)
    full_pair = last_owner // 2
    pair_ids = jnp.arange(pair_count, dtype=jnp.int32)
    pair_sizes = jnp.where(pair_ids == full_pair, N_TENSOR, pair_sizes).astype(jnp.int32)
    flipped = jnp.logical_and(pair_ids == full_pair, last_owner % 2 == 1)
    rank_keys = jax.random.split(jax.random.fold_in(mat_key, 3), pair_count)
    pair_ranks = jax.vmap(lambda sub_key: jax.random.permutation(sub_key, N_TENSOR))(rank_keys).astype(jnp.int32)
    members = pair_ranks < pair_sizes[:, None]
    first_side = jnp.logical_xor(members, flipped[:, None])
    owners = 2 * pair_ids[:, None] + jnp.where(first_side, 0, 1)
    slot_pos = jnp.where(members, pair_ranks, pair_ranks - pair_sizes[:, None])
    cell_keys = jax.random.split(jax.random.fold_in(mat_key, 4), N_TENSOR)
    cell_perm = jax.vmap(lambda sub_key: jax.random.permutation(sub_key, N_TENSOR * CAP))(cell_keys).astype(jnp.int32)
    slot_ids = jnp.arange(CAP, dtype=jnp.int32)
    raw_cell = slot_pos[:, :, None] * CAP + slot_ids[None, None, :]
    owner_full = jnp.broadcast_to(owners[:, :, None], raw_cell.shape)
    cells_at = cell_perm[owner_full, raw_cell]
    local_col = cells_at // DB
    row_block = cells_at % DB
    col_block = owner_full * OWN + local_col
    row_block = row_block.transpose(1, 0, 2).reshape(N_TENSOR, NNZ_DEV)
    col_block = col_block.transpose(1, 0, 2).reshape(N_TENSOR, NNZ_DEV)
    return (row_block, col_block)


def draw_gate_up_index(key, part):
    row_block, col_block = block_layout(key, 21)
    return jnp.stack([row_block, col_block], axis=-1).astype(jnp.int32)


def draw_down_index(key, part):
    row_block, col_block = block_layout(key, 31)
    return jnp.stack([col_block, row_block], axis=-1).astype(jnp.int32)


def steps_of(rng, shape, shards, least, high):
    level, own = 1.0, jax.random.fold_in(rng, 6)
    for position, shards_of in shards:
        draws = jnp.exp(jax.random.uniform(jax.random.fold_in(own, position), (shards_of,), jnp.float32, least / len(shards), high / len(shards)))
        level = level * jnp.repeat(draws, shape[position] // shards_of).reshape([-1 if axis == position else 1 for axis in range(len(shape))])
    return level


def bell_draw(own_key, extent, deviation, reach, shards=(), kind=jnp.bfloat16):
    entries = jax.random.normal(own_key, extent, jnp.float32) * deviation
    if len(shards) > 0:
        entries = steps_of(own_key, extent, shards, -0.22, 0.18) * entries
    return jnp.clip(entries, min=-reach, max=reach).astype(kind)


def setup_inputs(seed: int = 0) -> dict:
    keys = jax.random.split(jax.random.key(seed), 8)
    return {
        "tokens_in": bell_draw(keys[0], (TOKENS, D), 1.0, 6.0, ((0, 4), (1, 64))),
        "out_grad": bell_draw(keys[1], (TOKENS, D), 1.0, 6.0, ((0, 4), (1, 64))),
        "gate_blocks": bell_draw(keys[2], (BLOCKS, BS, BS), (D // 2) ** -0.5, 0.125, ((0, 64),)),
        "up_blocks": bell_draw(keys[3], (BLOCKS, BS, BS), (D // 2) ** -0.5, 0.125, ((0, 64),)),
        "down_blocks": bell_draw(keys[4], (BLOCKS, BS, BS), (FF // 2) ** -0.5, 0.0625, ((0, 64),)),
        "gate_up_index": draw_gate_up_index(jax.random.fold_in(keys[7], 71), 0),
        "down_index": draw_down_index(jax.random.fold_in(keys[7], 71), 0),
    }


def group_sum(left_rows, right_rows):
    count = left_rows.shape[0]
    lhs_blocks = left_rows.reshape(count, N_DP, TOK_DEV, BS)
    rhs_blocks = right_rows.reshape(count, N_DP, TOK_DEV, BS)
    part_sums = jnp.einsum("nqtk,nqtf->qnkf", lhs_blocks, rhs_blocks)
    rounded = lax.optimization_barrier(part_sums.astype(jnp.bfloat16))
    return jnp.sum(rounded.astype(jnp.float32), axis=0).astype(jnp.bfloat16)


def reference(tokens_in, out_grad, gate_blocks, up_blocks, down_blocks, gate_up_index, down_index):
    count_tok = tokens_in.shape[0]
    gu_list = gate_up_index.reshape(-1, 2).astype(jnp.int32)
    dn_list = down_index.reshape(-1, 2).astype(jnp.int32)
    gate_w = gate_blocks.astype(jnp.float32)
    up_w = up_blocks.astype(jnp.float32)
    down_w = down_blocks.astype(jnp.float32)
    x_blocks = tokens_in.reshape(count_tok, DB, BS).transpose(1, 0, 2)
    x_sel = jnp.take(x_blocks, gu_list[:, 0], axis=0).astype(jnp.float32)
    gate_sum = jax.ops.segment_sum(jnp.einsum("ntk,nkf->ntf", x_sel, gate_w), gu_list[:, 1], FB)
    up_sum = jax.ops.segment_sum(jnp.einsum("ntk,nkf->ntf", x_sel, up_w), gu_list[:, 1], FB)
    gate_sig = jax.nn.sigmoid(gate_sum)
    gate_act = gate_sum * gate_sig
    hidden = (gate_act * up_sum).astype(jnp.bfloat16)
    h_sel = jnp.take(hidden, dn_list[:, 0], axis=0).astype(jnp.float32)
    out_sum = jax.ops.segment_sum(jnp.einsum("ntk,nkf->ntf", h_sel, down_w), dn_list[:, 1], DB)
    output = out_sum.transpose(1, 0, 2).reshape(count_tok, D).astype(jnp.bfloat16)
    dy_blocks = out_grad.reshape(count_tok, DB, BS).transpose(1, 0, 2)
    dy_sel = jnp.take(dy_blocks, dn_list[:, 1], axis=0).astype(jnp.float32)
    hidden_grad = jax.ops.segment_sum(jnp.einsum("ntf,nkf->ntk", dy_sel, down_w), dn_list[:, 0], FB)
    gate_grad = (hidden_grad * up_sum * gate_sig * (1.0 + gate_sum * (1.0 - gate_sig))).astype(jnp.bfloat16)
    up_grad = (hidden_grad * gate_act).astype(jnp.bfloat16)
    g_sel = jnp.take(gate_grad, gu_list[:, 1], axis=0).astype(jnp.float32)
    u_sel = jnp.take(up_grad, gu_list[:, 1], axis=0).astype(jnp.float32)
    in_terms = jnp.einsum("ntf,nkf->ntk", g_sel, gate_w) + jnp.einsum("ntf,nkf->ntk", u_sel, up_w)
    in_sum = jax.ops.segment_sum(in_terms, gu_list[:, 0], DB)
    in_grad = in_sum.transpose(1, 0, 2).reshape(count_tok, D).astype(jnp.bfloat16)
    gate_grads = group_sum(x_sel, g_sel)
    up_grads = group_sum(x_sel, u_sel)
    down_grads = group_sum(h_sel, dy_sel)
    return (output, in_grad, gate_grads, up_grads, down_grads)
```

```python
import functools

import jax
import jax.numpy as jnp
from jax import lax
from jax.experimental import pallas as pl
from jax.experimental.pallas import tpu as pltpu
from jax.sharding import PartitionSpec as P

MESH = pl.DeviceIdType.MESH
BF = jnp.bfloat16
F32 = jnp.float32


def route_tables(lists, own, width_blocks, me):
    key = jnp.stack([k for k, _ in lists])
    other = jnp.stack([o for _, o in lists])
    nt, ne = key.shape[1:]
    owner = key // own
    cell = (key % own) * width_blocks + other
    my_owner = lax.dynamic_index_in_dim(owner, me, 1, keepdims=False)
    hit = my_owner[:, None, :] == jnp.arange(nt)[None, :, None]
    send = jnp.min(jnp.where(hit, jnp.arange(ne)[None, None, :], ne), axis=2)
    ret = jnp.max(jnp.where(owner == me, cell, -1), axis=2)
    match = ret[:, None, :] == jnp.arange(own * width_blocks)[None, :, None]
    source = jnp.min(jnp.where(match, jnp.arange(nt)[None, None, :], nt), axis=2)
    table = jnp.concatenate([send, source, jnp.maximum(ret, 0), my_owner], axis=1)
    return table.astype(jnp.int32).reshape(-1)


def kernel(
    cfg,
    idx,
    x_ref,
    dy_ref,
    gate_hbm,
    up_hbm,
    down_hbm,
    out_ref,
    in_ref,
    gg_ref,
    ug_ref,
    dg_ref,
    gu_in,
    dn_in,
    dn_t,
    xs,
    ws_gu,
    wr_gu,
    ws_dn,
    wr_dn,
    xall,
    wd,
    part,
    psum_in,
    hid,
    oall,
    c_in,
    tsum,
    y_in,
    usum,
    z_in,
    vsum,
    f_in,
    gc,
    gd,
    gs_gu,
    gr_gu,
    gs_dn,
    gr_dn,
    zl,
    zs,
    zr,
    load_sem,
    dpx_s,
    dpx_r,
    zg_s,
    zg_r,
    yg_s,
    yg_r,
    cg_s,
    cg_r,
    wdn_s,
    wdn_r,
    wgu_s,
    wgu_r,
    ph_s,
    ph_r,
    pg_s,
    pg_r,
    h_s,
    h_r,
    co_s,
    co_r,
    yo_s,
    yo_r,
    zo_s,
    zo_r,
    fo_s,
    fo_r,
    gdn_s,
    gdn_r,
    ggu_s,
    ggu_r,
    zx_s,
    zx_r,
):
    nx, ny, nz, ne, own, db = cfg
    nt = ny * nz * 2
    npl = ny * nz
    bs = 128
    tk = 128
    rr = bs // nx
    dpc = nx // 2
    fown = own * bs
    cells = own * db
    stride = nt + cells + nt + ne
    d = lax.axis_index("dp")
    t = lax.axis_index("tensor")
    c = t % 2
    chip = t // 2
    y = chip // nz
    z = chip % nz

    def dev(dd, tt):
        return (dd, tt)

    def rcopy(src, dst, ssem, rsem, dd, tt):
        return pltpu.make_async_remote_copy(
            src_ref=src,
            dst_ref=dst,
            send_sem=ssem,
            recv_sem=rsem,
            device_id=dev(dd, tt),
            device_id_type=MESH,
        )

    barrier = pltpu.get_barrier_semaphore()

    @pl.loop(1, nt)
    def _(i):
        pl.semaphore_signal(
            barrier, inc=1, device_id=dev(d, lax.rem(t + i, nt)), device_id_type=MESH
        )

    for k in range(1, nx):
        for cc in range(2):
            pl.semaphore_signal(
                barrier,
                inc=1,
                device_id=dev(lax.rem(d + k, nx), chip * 2 + cc),
                device_id_type=MESH,
            )

    rows = pl.ds(pl.multiple_of(d * rr, rr), rr)
    loads = [
        pltpu.make_async_copy(gate_hbm.at[:, rows, :], gu_in.at[0, pl.ds(0, ne)], load_sem.at[0]),
        pltpu.make_async_copy(up_hbm.at[:, rows, :], gu_in.at[1, pl.ds(0, ne)], load_sem.at[1]),
        pltpu.make_async_copy(down_hbm, dn_in, load_sem.at[2]),
    ]
    for cp in loads:
        cp.start()

    half = x_ref.shape[1]
    eye = (
        lax.broadcasted_iota(jnp.int32, (half, half), 0)
        == lax.broadcasted_iota(jnp.int32, (half, half), 1)
    ).astype(F32).astype(BF)
    nt_dims = (((1,), (1,)), ((), ()))
    for a, ref in enumerate((x_ref, dy_ref)):
        xt = lax.dot_general(eye, ref[...], nt_dims, preferred_element_type=F32)
        xs[a] = xt.astype(BF).reshape(dpc, rr, tk)

    zero_rows = jnp.zeros((rr, bs), BF)
    gu_in[0, ne] = zero_rows
    gu_in[1, ne] = zero_rows
    dn_t[ne] = zero_rows
    wr_gu[nt, 0] = zero_rows
    wr_gu[nt, 1] = zero_rows
    wr_dn[nt] = zero_rows

    loads[2].wait()
    pick = (
        lax.broadcasted_iota(jnp.int32, (rr, bs), 1)
        == lax.broadcasted_iota(jnp.int32, (rr, bs), 0) + d * rr
    ).astype(F32).astype(BF)

    @pl.loop(0, ne)
    def _(e):
        dn_t[e] = lax.dot_general(
            pick, dn_in[e], nt_dims, preferred_element_type=F32
        ).astype(BF)

    @pl.loop(0, nt)
    def _(s):
        ws_dn[s] = dn_t[idx[stride + s]]

    wr_dn[t] = ws_dn[t]
    loads[0].wait()
    loads[1].wait()

    @pl.loop(0, nt)
    def _(s):
        e = idx[s]
        ws_gu[s, 0] = gu_in[0, e]
        ws_gu[s, 1] = gu_in[1, e]

    wr_gu[t] = ws_gu[t]

    pl.semaphore_wait(barrier, nt - 1 + 2 * (nx - 1))

    def dpx(a, j, go):
        dst_d = c * dpc + j
        is_me = jnp.logical_and(dst_d == d, c == a)

        @pl.when(jnp.logical_not(is_me))
        def _():
            go(
                rcopy(
                    xs.at[a, j],
                    xall.at[a, chip, :, pl.ds(pl.multiple_of(d * tk, tk), tk)],
                    dpx_s.at[a, j],
                    dpx_r.at[d],
                    dst_d,
                    chip * 2 + a,
                )
            )

    for a in range(2):
        for j in range(dpc):
            dpx(a, j, lambda cp: cp.start())

    @pl.when(d // dpc == c)
    def _():
        xall[c, chip, :, pl.ds(pl.multiple_of(d * tk, tk), tk)] = xs[c, d % dpc]

    def a2a(src, dst, ssem, rsem, lo, hi):
        @pl.loop(lo, hi)
        def _(i):
            to = lax.rem(t + i, nt)
            rcopy(src.at[to], dst.at[t], ssem, rsem, d, to).start()

    def a2a_wait(src, dst, ssem, rsem, what):
        cp = rcopy(
            src.at[pl.ds(0, nt - 1)], dst.at[pl.ds(0, nt - 1)], ssem, rsem, d, lax.rem(t + 1, nt)
        )
        if what == "send":
            cp.wait_send()
        else:
            cp.wait_recv()

    a2a(ws_dn, wr_dn, wdn_s, wdn_r, 1, nt)

    for q in range(nx):

        @pl.when(jnp.logical_not(jnp.logical_and(q == d, d // dpc == c)))
        def _():
            rcopy(
                xs.at[0, 0],
                xall.at[c, chip, :, pl.ds(q * tk, tk)],
                dpx_s.at[0, 0],
                dpx_r.at[q],
                d,
                lax.rem(t + 1, nt),
            ).wait_recv()

    def zg(k):
        zz = lax.rem(z + k, nz)
        return rcopy(
            xall.at[c, chip],
            xall.at[c, chip],
            zg_s.at[k],
            zg_r.at[k],
            d,
            (y * nz + zz) * 2 + c,
        )

    for k in range(1, nz):
        zg(k).start()

    mid = nt // 2
    a2a(ws_gu, wr_gu, wgu_s, wgu_r, 1, mid)
    for k in range(1, nz):
        src_z = lax.rem(z - k + nz, nz)
        rcopy(
            xall.at[c, chip],
            xall.at[c, y * nz + src_z],
            zg_s.at[k],
            zg_r.at[k],
            d,
            lax.rem(t + 1, nt),
        ).wait_recv()

    def row_of(yy):
        return pl.ds(yy * nz, nz)

    for k in range(1, ny):
        yy = lax.rem(y + k, ny)
        rcopy(
            xall.at[c, row_of(y)],
            xall.at[c, row_of(y)],
            yg_s.at[k],
            yg_r.at[k],
            d,
            (yy * nz + z) * 2 + c,
        ).start()

    def to_core(k):
        yy = lax.rem(y - k + ny, ny)
        return rcopy(
            xall.at[c, row_of(yy)],
            xall.at[c, row_of(yy)],
            cg_s.at[k],
            cg_r.at[k],
            d,
            chip * 2 + 1 - c,
        )

    to_core(0).start()
    a2a(ws_gu, wr_gu, wgu_s, wgu_r, mid, nt)
    for k in range(1, ny):
        yy = lax.rem(y - k + ny, ny)
        rcopy(
            xall.at[c, row_of(y)],
            xall.at[c, row_of(yy)],
            yg_s.at[k],
            yg_r.at[k],
            d,
            lax.rem(t + 1, nt),
        ).wait_recv()
        to_core(k).start()
    for k in range(ny):
        yy = lax.rem(y - k + ny, ny)
        rcopy(
            xall.at[c, row_of(yy)],
            xall.at[1 - c, row_of(yy)],
            cg_s.at[k],
            cg_r.at[k],
            d,
            chip * 2 + 1 - c,
        ).wait_recv()

    a2a_wait(ws_dn, wr_dn, wdn_s, wdn_r, "recv")

    @pl.loop(0, db)
    def _(a):
        for jl in range(own):
            s = idx[stride + nt + jl * db + a]
            wd[a, :, pl.ds(2 * fown + jl * bs, bs)] = wr_dn[s]

    tn_dims = (((0,), (0,)), ((), ()))
    kall = db * rr
    tok = nx * tk

    def partials(lo, hi, arr):
        @pl.loop(lo, hi)
        def _(f):
            cols = pl.ds(pl.multiple_of(f * bs, bs), bs)
            lhs = wd[:, :, cols].reshape(kall, bs)
            rhs = xall[arr].reshape(kall, tok)
            res = lax.dot_general(lhs, rhs, tn_dims, preferred_element_type=F32)
            part[pl.ds(pl.multiple_of(f * bs, bs), bs), :] = res.astype(BF)

    def dp_out(lo, size, k, ssem, rsem):
        dd = lax.rem(d + k, nx)
        return rcopy(
            part.at[pl.ds(lo, size), pl.ds(pl.multiple_of(dd * tk, tk), tk)],
            psum_in.at[k, pl.ds(lo, size), :],
            ssem.at[k],
            rsem.at[k],
            dd,
            t,
        )

    partials(2 * own, 3 * own, 1)
    for k in range(1, nx):
        dp_out(2 * fown, fown, k, ph_s, ph_r).start()

    a2a_wait(ws_gu, wr_gu, wgu_s, wgu_r, "recv")

    @pl.loop(0, db)
    def _(a):
        for jl in range(own):
            s = idx[nt + jl * db + a]
            wd[a, :, pl.ds(jl * bs, bs)] = wr_gu[s, 0]
            wd[a, :, pl.ds(fown + jl * bs, bs)] = wr_gu[s, 1]

    partials(0, 2 * own, 0)
    for k in range(1, nx):
        dp_out(0, 2 * fown, k, pg_s, pg_r).start()
    for k in range(1, nx):
        dp_out(2 * fown, fown, k, ph_s, ph_r).wait_recv()
        dp_out(0, 2 * fown, k, pg_s, pg_r).wait_recv()

    my_tok = pl.ds(pl.multiple_of(d * tk, tk), tk)

    @pl.loop(0, own)
    def _(j):
        def total(base):
            r = pl.ds(pl.multiple_of(base + j * bs, bs), bs)
            acc = part[r, my_tok].astype(F32)
            for k in range(1, nx):
                acc += psum_in[k, r, :].astype(F32)
            return acc

        gate = total(0)
        up = total(fown)
        hg = total(2 * fown)
        sig = 1.0 / (1.0 + jnp.exp(-gate))
        act = gate * sig
        hid[pl.ds(pl.multiple_of(2 * fown + j * bs, bs), bs), my_tok] = (act * up).astype(BF)
        hid[pl.ds(pl.multiple_of(j * bs, bs), bs), my_tok] = (
            hg * up * sig * (1.0 + gate * (1.0 - sig))
        ).astype(BF)
        hid[pl.ds(pl.multiple_of(fown + j * bs, bs), bs), my_tok] = (hg * act).astype(BF)

    for k in range(1, nx):
        rcopy(
            hid.at[:, my_tok], hid.at[:, my_tok], h_s.at[k], h_r.at[k], lax.rem(d + k, nx), t
        ).start()
    for k in range(1, nx):
        src = lax.rem(d - k + nx, nx)
        rcopy(
            hid.at[:, my_tok],
            hid.at[:, pl.ds(pl.multiple_of(src * tk, tk), tk)],
            h_s.at[k],
            h_r.at[k],
            src,
            t,
        ).wait_recv()

    mt = 256 // rr

    @pl.loop(0, db // mt)
    def _(i):
        a0 = i * mt
        arows = pl.ds(a0, mt)
        for dst, lo, size in ((0, 2 * fown, fown), (1, 0, 2 * fown)):
            lhs = wd[arows, :, pl.ds(lo, size)].reshape(mt * rr, size)
            res = jnp.dot(lhs, hid[pl.ds(lo, size), :], preferred_element_type=F32)
            oall[dst, arows] = res.astype(BF).reshape(mt, rr, tok)

    other = chip * 2 + 1 - c
    core_out = rcopy(oall.at[1 - c], c_in, co_s, co_r, d, other)
    core_out.start()

    def grads(arr, lo, size):
        def body(i, store):
            lhs = xall[arr, pl.ds(i * mt, mt)].reshape(mt * rr, tok)
            res = lax.dot_general(
                lhs, hid[pl.ds(lo, size), :], nt_dims, preferred_element_type=F32
            )
            store(i * mt, res.astype(BF))

        return body

    def store_dn(a0, res):
        for jl in range(own):
            gd[pl.ds(jl * db + a0, mt)] = res[:, jl * bs : (jl + 1) * bs].reshape(mt, rr, bs)

    def store_gu(a0, res):
        for h in range(2):
            for jl in range(own):
                lo = h * fown + jl * bs
                gc[pl.ds(jl * db + a0, mt), h] = res[:, lo : lo + bs].reshape(mt, rr, bs)

    @pl.loop(0, db // mt)
    def _(i):
        grads(1, 2 * fown, fown)(i, store_dn)

    @pl.loop(0, nt)
    def _(s):
        gs_dn[s] = gd[idx[stride + nt + cells + s]]

    gr_dn[t] = gs_dn[t]
    a2a(gs_dn, gr_dn, gdn_s, gdn_r, 1, nt)

    @pl.loop(0, db // mt)
    def _(i):
        grads(0, 0, 2 * fown)(i, store_gu)

    @pl.loop(0, nt)
    def _(s):
        gs_gu[s] = gc[idx[nt + cells + s]]

    gr_gu[t] = gs_gu[t]

    core_out.wait_recv()

    @pl.loop(0, npl)
    def _(p):
        tsum[p] = (oall[c, p].astype(F32) + c_in[p].astype(F32)).astype(BF)

    for k in range(1, ny):
        yy = lax.rem(y + k, ny)
        rcopy(
            tsum.at[row_of(yy)], y_in.at[k], yo_s.at[k], yo_r.at[k], d, (yy * nz + z) * 2 + c
        ).start()
    a2a(gs_gu, gr_gu, ggu_s, ggu_r, 1, nt)
    for k in range(1, ny):
        rcopy(tsum.at[row_of(y)], y_in.at[k], yo_s.at[k], yo_r.at[k], d, other).wait_recv()

    @pl.loop(0, nz)
    def _(p):
        acc = tsum[y * nz + p].astype(F32)
        for k in range(1, ny):
            acc += y_in[k, p].astype(F32)
        usum[p] = acc.astype(BF)

    for k in range(1, nz):
        zz = lax.rem(z + k, nz)
        rcopy(
            usum.at[zz], z_in.at[k], zo_s.at[k], zo_r.at[k], d, (y * nz + zz) * 2 + c
        ).start()

    a2a_wait(gs_dn, gr_dn, gdn_s, gdn_r, "recv")
    groups = ne // nx

    @pl.loop(0, groups)
    def _(g):
        for p in range(nx):
            o = idx[stride + nt + cells + nt + g * nx + p]
            zl[g, :, pl.ds(p * bs, bs)] = gr_dn[o]

    lane = lax.broadcasted_iota(jnp.int32, (nx * bs, bs), 0)
    col = lax.broadcasted_iota(jnp.int32, (nx * bs, bs), 1)
    for dd in range(nx):
        want = (col // rr) * bs + dd * rr + col % rr
        perm = (lane == want).astype(F32).astype(BF)
        moved = jnp.dot(zl[...].reshape(groups * rr, nx * bs), perm, preferred_element_type=F32)
        zs[dd] = moved.astype(BF).reshape(groups, rr, bs)
    zr[d] = zs[d]
    for k in range(1, nx):
        dd = lax.rem(d + k, nx)
        rcopy(zs.at[dd], zr.at[d], zx_s.at[k], zx_r.at[k], dd, t).start()

    for k in range(1, nz):
        rcopy(usum.at[z], z_in.at[k], zo_s.at[k], zo_r.at[k], d, other).wait_recv()
    acc = usum[z].astype(F32)
    for k in range(1, nz):
        acc += z_in[k].astype(F32)
    vsum[...] = acc.astype(BF)

    fcore = chip * 2 + d // dpc

    def is_self(q):
        return jnp.logical_and(q == d, d // dpc == c)

    for q in range(nx):

        @pl.when(jnp.logical_not(is_self(q)))
        def _():
            rcopy(
                vsum.at[:, pl.ds(q * tk, tk)],
                f_in.at[c, d % dpc],
                fo_s.at[q],
                fo_r.at[c, d % dpc],
                q,
                fcore,
            ).start()

    @pl.when(d // dpc == c)
    def _():
        f_in[c, d % dpc] = vsum[:, my_tok]

    for k in range(1, nx):
        src = lax.rem(d - k + nx, nx)
        rcopy(zs.at[0], zr.at[src], zx_s.at[k], zx_r.at[k], src, t).wait_recv()
    eye_b = (
        lax.broadcasted_iota(jnp.int32, (bs, bs), 0) == lax.broadcasted_iota(jnp.int32, (bs, bs), 1)
    ).astype(F32).astype(BF)

    @pl.loop(0, groups)
    def _(g):
        block = zr[:, g].reshape(nx * rr, bs)
        flip = lax.dot_general(block, eye_b, tn_dims, preferred_element_type=F32)
        dg_ref[pl.ds(g * nx, nx)] = flip.astype(BF).reshape(nx, rr, bs)

    for a in range(2):
        for j in range(dpc):
            src_d = c * dpc + j
            own_piece = jnp.logical_and(src_d == d, a == c)

            @pl.when(jnp.logical_not(own_piece))
            def _():
                rcopy(
                    vsum.at[:, pl.ds(0, tk)],
                    f_in.at[a, j],
                    fo_s.at[0],
                    fo_r.at[a, j],
                    src_d,
                    other,
                ).wait_recv()

    for a, ref in enumerate((out_ref, in_ref)):
        block = f_in[a].reshape(half, tk)
        ref[...] = lax.dot_general(
            eye_b, block, nt_dims, preferred_element_type=F32
        ).astype(BF)

    a2a_wait(gs_gu, gr_gu, ggu_s, ggu_r, "recv")

    @pl.loop(0, ne)
    def _(e):
        o = idx[nt + cells + nt + e]
        gg_ref[e] = gr_gu[o, 0]
        ug_ref[e] = gr_gu[o, 1]

    for a in range(2):
        for j in range(dpc):
            dpx(a, j, lambda cp: cp.wait_send())
    a2a_wait(ws_dn, wr_dn, wdn_s, wdn_r, "send")
    a2a_wait(ws_gu, wr_gu, wgu_s, wgu_r, "send")
    a2a_wait(gs_dn, gr_dn, gdn_s, gdn_r, "send")
    a2a_wait(gs_gu, gr_gu, ggu_s, ggu_r, "send")
    for k in range(1, nz):
        zg(k).wait_send()
        rcopy(usum.at[z], z_in.at[k], zo_s.at[k], zo_r.at[k], d, other).wait_send()
    for k in range(1, ny):
        rcopy(
            xall.at[c, row_of(y)], xall.at[c, row_of(y)], yg_s.at[k], yg_r.at[k], d, other
        ).wait_send()
        rcopy(tsum.at[row_of(y)], y_in.at[k], yo_s.at[k], yo_r.at[k], d, other).wait_send()
    for k in range(ny):
        to_core(k).wait_send()
    for k in range(1, nx):
        dp_out(2 * fown, fown, k, ph_s, ph_r).wait_send()
        dp_out(0, 2 * fown, k, pg_s, pg_r).wait_send()
        rcopy(hid.at[:, my_tok], hid.at[:, my_tok], h_s.at[k], h_r.at[k], d, other).wait_send()
        rcopy(zs.at[0], zr.at[0], zx_s.at[k], zx_r.at[k], d, other).wait_send()
    core_out.wait_send()
    for q in range(nx):

        @pl.when(jnp.logical_not(is_self(q)))
        def _():
            rcopy(
                vsum.at[:, pl.ds(q * tk, tk)],
                f_in.at[c, d % dpc],
                fo_s.at[q],
                fo_r.at[c, d % dpc],
                q,
                fcore,
            ).wait_send()


def per_device(dims, tokens_in, out_grad, gate_blocks, up_blocks, down_blocks, gate_up_index, down_index):
    nx, ny, nz = dims
    nt, ne = gate_up_index.shape[:2]
    npl = ny * nz
    db = npl
    bs = gate_blocks.shape[1]
    tk = tokens_in.shape[0]
    own = dims_own(dims)
    rr = bs // nx
    dpc = nx // 2
    fown = own * bs
    tok = nx * tk
    cells = own * db
    me = lax.axis_index("tensor")
    tables = route_tables(
        (
            (gate_up_index[:, :, 1], gate_up_index[:, :, 0]),
            (down_index[:, :, 0], down_index[:, :, 1]),
        ),
        own,
        db,
        me,
    )
    v = lambda *s: pltpu.VMEM(s, BF)
    dma = lambda *s: pltpu.SemaphoreType.DMA(s)
    scratch = [
        v(2, ne + 1, rr, bs),
        v(ne, bs, bs),
        v(ne + 1, rr, bs),
        v(2, dpc, rr, tk),
        v(nt, 2, rr, bs),
        v(nt + 1, 2, rr, bs),
        v(nt, rr, bs),
        v(nt + 1, rr, bs),
        v(2, npl, rr, tok),
        v(db, rr, 3 * fown),
        v(3 * fown, tok),
        v(nx, 3 * fown, tk),
        v(3 * fown, tok),
        v(2, npl, rr, tok),
        v(npl, rr, tok),
        v(npl, rr, tok),
        v(ny, nz, rr, tok),
        v(nz, rr, tok),
        v(nz, rr, tok),
        v(rr, tok),
        v(2, dpc, rr, tk),
        v(cells, 2, rr, bs),
        v(cells, rr, bs),
        v(nt, 2, rr, bs),
        v(nt, 2, rr, bs),
        v(nt, rr, bs),
        v(nt, rr, bs),
        v(ne // nx, rr, nx * bs),
        v(nx, ne // nx, rr, bs),
        v(nx, ne // nx, rr, bs),
        dma(3),
        dma(2, dpc),
        dma(nx),
        dma(nz),
        dma(nz),
        dma(ny),
        dma(ny),
        dma(ny),
        dma(ny),
        pltpu.SemaphoreType.DMA,
        pltpu.SemaphoreType.DMA,
        pltpu.SemaphoreType.DMA,
        pltpu.SemaphoreType.DMA,
        dma(nx),
        dma(nx),
        dma(nx),
        dma(nx),
        dma(nx),
        dma(nx),
        pltpu.SemaphoreType.DMA,
        pltpu.SemaphoreType.DMA,
        dma(ny),
        dma(ny),
        dma(nz),
        dma(nz),
        dma(nx),
        dma(2, dpc),
        pltpu.SemaphoreType.DMA,
        pltpu.SemaphoreType.DMA,
        pltpu.SemaphoreType.DMA,
        pltpu.SemaphoreType.DMA,
        dma(nx),
        dma(nx),
    ]
    vm = pl.BlockSpec(memory_space=pltpu.VMEM)
    hbm = pl.BlockSpec(memory_space=pl.ANY)
    grad = jax.ShapeDtypeStruct((ne, rr, bs), BF)
    act = jax.ShapeDtypeStruct(tokens_in.shape, BF)
    return pl.pallas_call(
        functools.partial(kernel, (nx, ny, nz, ne, own, db)),
        out_shape=(act, act, grad, grad, grad),
        in_specs=[pl.BlockSpec(memory_space=pltpu.SMEM), vm, vm, hbm, hbm, hbm],
        out_specs=(vm,) * 5,
        scratch_shapes=scratch,
        compiler_params=pltpu.CompilerParams(
            collective_id=0, has_side_effects=True, vmem_limit_bytes=56 * 2**20
        ),
    )(tables, tokens_in, out_grad, gate_blocks, up_blocks, down_blocks)


FB = 128
GRID = {4: (4, 8)}


def dims_own(dims):
    return FB // (dims[1] * dims[2] * 2)


def solution(mesh):
    nx, nt = mesh.shape["dp"], mesh.shape["tensor"]
    ny, nz = GRID[nx]
    in_specs = (
        P("dp", "tensor"),
        P("dp", "tensor"),
        P("tensor", None, None),
        P("tensor", None, None),
        P("tensor", None, None),
        P(),
        P(),
    )
    out_specs = (
        P("dp", "tensor"),
        P("dp", "tensor"),
        P("tensor", "dp", None),
        P("tensor", "dp", None),
        P("tensor", "dp", None),
    )
    return jax.shard_map(
        functools.partial(per_device, (nx, ny, nz)),
        mesh=mesh,
        in_specs=in_specs,
        out_specs=out_specs,
        check_vma=False,
    )
```

```python
import functools

import jax
import jax.numpy as jnp
from jax import lax
from jax.experimental import pallas as pl
from jax.experimental.pallas import tpu as pltpu
from jax.sharding import PartitionSpec as P

MESH = pl.DeviceIdType.MESH
BF = jnp.bfloat16
F32 = jnp.float32


def route_tables(lists, own, width_blocks, me):
    key = jnp.stack([k for k, _ in lists])
    other = jnp.stack([o for _, o in lists])
    nt, ne = key.shape[1:]
    owner = key // own
    cell = (key % own) * width_blocks + other
    my_owner = lax.dynamic_index_in_dim(owner, me, 1, keepdims=False)
    hit = my_owner[:, None, :] == jnp.arange(nt)[None, :, None]
    send = jnp.min(jnp.where(hit, jnp.arange(ne)[None, None, :], ne), axis=2)
    ret = jnp.max(jnp.where(owner == me, cell, -1), axis=2)
    match = ret[:, None, :] == jnp.arange(own * width_blocks)[None, :, None]
    source = jnp.min(jnp.where(match, jnp.arange(nt)[None, None, :], nt), axis=2)
    table = jnp.concatenate([send, source, jnp.maximum(ret, 0), my_owner], axis=1)
    return table.astype(jnp.int32).reshape(-1)


def kernel(
    cfg,
    idx,
    x_hbm,
    dy_hbm,
    gate_hbm,
    up_hbm,
    down_hbm,
    out_ref,
    in_ref,
    gg_ref,
    ug_ref,
    dg_ref,
    gu_in,
    gu_ab,
    dn_in,
    dn_t,
    xs,
    ws_gu,
    wr_a,
    wr_b,
    ws_dn,
    wr_dn,
    xall,
    wd,
    part,
    psum_in,
    part_d,
    psum_d,
    hid_g,
    hid_d,
    oall,
    c_in,
    tsum,
    y_in,
    usum,
    z_in,
    vsum,
    f_in,
    gc,
    gd,
    gs_gu,
    gr_gu,
    gs_dn,
    gr_dn,
    stage,
    zl,
    zs,
    zr,
    load_sem,
    dpx_s,
    dpx_r,
    zg_s,
    zg_r,
    yg_s,
    yg_r,
    cg_s,
    cg_r,
    wdn_s,
    wdn_r,
    wgu_s,
    wgu_r,
    ph_s,
    ph_r,
    pd_s,
    pd_r,
    hg_s,
    hg_r,
    hd_s,
    hd_r,
    co_s,
    co_r,
    yo_s,
    yo_r,
    zo_s,
    zo_r,
    fo_s,
    fo_r,
    gdn_s,
    gdn_r,
    ggu_s,
    ggu_r,
    zx_s,
    zx_r,
):
    nx, ny, nz, ne, own, db = cfg
    wr_gu = (wr_a, wr_b)
    nt = ny * nz * 2
    npl = ny * nz
    bs = 128
    hb = bs // 2
    tk = 128
    rr = bs // nx
    dpc = nx // 2
    fown = own * bs
    cells = own * db
    stride = nt + cells + nt + ne
    tok = nx * tk
    kall = db * rr
    d = lax.axis_index("dp")
    t = lax.axis_index("tensor")
    c = t % 2
    chip = t // 2
    y = chip // nz
    z = chip % nz
    other = chip * 2 + 1 - c
    my_tok = pl.ds(pl.multiple_of(d * tk, tk), tk)
    nt_dims = (((1,), (1,)), ((), ()))
    tn_dims = (((0,), (0,)), ((), ()))

    def onehot(shape, fn):
        return fn(
            lax.broadcasted_iota(jnp.int32, shape, 0), lax.broadcasted_iota(jnp.int32, shape, 1)
        ).astype(F32).astype(BF)

    def rcopy(src, dst, ssem, rsem, dd, tt):
        return pltpu.make_async_remote_copy(
            src_ref=src,
            dst_ref=dst,
            send_sem=ssem,
            recv_sem=rsem,
            device_id=(dd, tt),
            device_id_type=MESH,
        )

    barrier = pltpu.get_barrier_semaphore()

    rows = pl.ds(pl.multiple_of(d * rr, rr), rr)
    loads = [
        pltpu.make_async_copy(gate_hbm.at[:, rows, :], gu_in.at[0], load_sem.at[0]),
        pltpu.make_async_copy(up_hbm.at[:, rows, :], gu_in.at[1], load_sem.at[1]),
        pltpu.make_async_copy(x_hbm, xs.at[0], load_sem.at[2]),
        pltpu.make_async_copy(dy_hbm, xs.at[1], load_sem.at[3]),
        pltpu.make_async_copy(down_hbm, dn_in, load_sem.at[4]),
    ]
    for cp in loads:
        cp.start()

    @pl.loop(1, nt)
    def _(i):
        pl.semaphore_signal(
            barrier, inc=1, device_id=(d, lax.rem(t + i, nt)), device_id_type=MESH
        )

    for k in range(1, nx):
        for cc in range(2):
            pl.semaphore_signal(
                barrier,
                inc=1,
                device_id=(lax.rem(d + k, nx), chip * 2 + cc),
                device_id_type=MESH,
            )

    zero_rows = jnp.zeros((rr, bs), BF)
    dn_t[ne] = zero_rows
    wr_dn[nt] = zero_rows
    for h in range(2):
        gu_ab[h, ne] = zero_rows
        wr_gu[h][nt] = zero_rows

    def half_src(i):
        return (i % bs) // hb * bs + i // bs * hb + i % hb

    halves = onehot((2 * bs, 2 * bs), lambda r, q: r == half_src(q))
    loads[0].wait()
    loads[1].wait()
    me_n = 256 // rr

    @pl.loop(0, ne // me_n)
    def _(i):
        es = pl.ds(i * me_n, me_n)
        both = jnp.concatenate(
            [gu_in[0, es].reshape(me_n * rr, bs), gu_in[1, es].reshape(me_n * rr, bs)], axis=1
        )
        res = jnp.dot(both, halves, preferred_element_type=F32).astype(BF)
        for h in range(2):
            gu_ab[h, es] = res[:, h * bs : (h + 1) * bs].reshape(me_n, rr, bs)

    @pl.loop(0, nt)
    def _(s):
        e = idx[s]
        ws_gu[0, s] = gu_ab[0, e]
        ws_gu[1, s] = gu_ab[1, e]

    for h in range(2):
        wr_gu[h][t] = ws_gu[h, t]

    loads[2].wait()
    loads[3].wait()
    pl.semaphore_wait(barrier, nt - 1 + 2 * (nx - 1))

    def dpx(a, j, go):
        dst_d = c * dpc + j
        is_me = jnp.logical_and(dst_d == d, c == a)

        @pl.when(jnp.logical_not(is_me))
        def _():
            go(
                rcopy(
                    xs.at[a, j],
                    xall.at[a, chip, :, my_tok],
                    dpx_s.at[a, j],
                    dpx_r.at[d],
                    dst_d,
                    chip * 2 + a,
                )
            )

    for a in range(2):
        for j in range(dpc):
            dpx(a, j, lambda cp: cp.start())

    @pl.when(d // dpc == c)
    def _():
        xall[c, chip, :, my_tok] = xs[c, d % dpc]

    def a2a(src, dst, ssem, rsem, lo, hi):
        @pl.loop(lo, hi)
        def _(i):
            to = lax.rem(t + i, nt)
            rcopy(src.at[to], dst.at[t], ssem, rsem, d, to).start()

    def a2a_all(src, dst, ssem, rsem):
        return rcopy(
            src.at[pl.ds(0, nt - 1)], dst.at[pl.ds(0, nt - 1)], ssem, rsem, d, lax.rem(t + 1, nt)
        )

    def gu_out(h):
        return ws_gu.at[h], wr_gu[h], wgu_s.at[h], wgu_r.at[h]

    dn_out = (ws_dn, wr_dn, wdn_s, wdn_r)
    mid = nt // 2

    loads[4].wait()
    pick = onehot((rr, bs), lambda r, q: q == r + d * rr)
    en = 8 if ne % 8 == 0 else ne

    @pl.loop(0, ne // en)
    def _(i):
        blocks = dn_in[pl.ds(i * en, en)].reshape(en * bs, bs)
        res = lax.dot_general(pick, blocks, nt_dims, preferred_element_type=F32).astype(BF)
        for k in range(en):
            dn_t[i * en + k] = res[:, k * bs : (k + 1) * bs]

    @pl.loop(0, nt)
    def _(s):
        ws_dn[s] = dn_t[idx[stride + s]]

    wr_dn[t] = ws_dn[t]

    for q in range(nx):

        @pl.when(jnp.logical_not(jnp.logical_and(q == d, d // dpc == c)))
        def _():
            rcopy(
                xs.at[0, 0],
                xall.at[c, chip, :, pl.ds(q * tk, tk)],
                dpx_s.at[0, 0],
                dpx_r.at[q],
                d,
                other,
            ).wait_recv()

    def zg(k):
        return rcopy(
            xall.at[c, chip],
            xall.at[c, chip],
            zg_s.at[k],
            zg_r.at[k],
            d,
            (y * nz + lax.rem(z + k, nz)) * 2 + c,
        )

    for k in range(1, nz):
        zg(k).start()
    a2a(*gu_out(0), 1, nt)


    for k in range(1, nz):
        rcopy(
            xall.at[c, chip],
            xall.at[c, y * nz + lax.rem(z - k + nz, nz)],
            zg_s.at[k],
            zg_r.at[k],
            d,
            other,
        ).wait_recv()

    def row_of(yy):
        return pl.ds(yy * nz, nz)

    def yg(k):
        yy = lax.rem(y + k, ny)
        return rcopy(
            xall.at[c, row_of(y)],
            xall.at[c, row_of(y)],
            yg_s.at[k],
            yg_r.at[k],
            d,
            (yy * nz + z) * 2 + c,
        )

    def to_core(k, arr):
        yy = lax.rem(y - k + ny, ny)
        return rcopy(
            xall.at[c, row_of(yy)], xall.at[arr, row_of(yy)], cg_s.at[k], cg_r.at[k], d, other
        )

    for k in range(1, ny):
        yg(k).start()
    to_core(0, c).start()
    a2a(*dn_out, 1, nt)

    for k in range(1, ny):
        yy = lax.rem(y - k + ny, ny)
        rcopy(
            xall.at[c, row_of(y)],
            xall.at[c, row_of(yy)],
            yg_s.at[k],
            yg_r.at[k],
            d,
            other,
        ).wait_recv()
        to_core(k, c).start()
    a2a(*gu_out(1), 1, nt)
    for k in range(ny):
        to_core(k, 1 - c).wait_recv()

    def partials(lo, arr, store):
        @pl.loop(0, own)
        def _(f):
            cols = pl.ds(pl.multiple_of(lo + f * bs, bs), bs)
            lhs = wd[:, :, cols].reshape(kall, bs)
            rhs = xall[arr].reshape(kall, tok)
            store(f, lax.dot_general(lhs, rhs, tn_dims, preferred_element_type=F32).astype(BF))

    def partials_gu(h):
        def store(f, res):
            part[h, pl.ds(pl.multiple_of(f * bs, bs), bs), :] = res

        partials((1 + h) * fown, 0, store)

    def store_hg(f, res):
        part_d[f] = res.reshape(2, hb, tok)

    def dp_out(h, k):
        dd = lax.rem(d + k, nx)
        dst_tok = pl.ds(pl.multiple_of(dd * tk, tk), tk)
        return (
            rcopy(
                part.at[h, :, dst_tok], psum_in.at[k, h], ph_s.at[h, k], ph_r.at[h, k], dd, t
            ),
            rcopy(
                part_d.at[:, h, :, dst_tok],
                psum_d.at[k, :, h],
                pd_s.at[h, k],
                pd_r.at[h, k],
                dd,
                t,
            ),
        )

    def dp_send(h):
        for k in range(1, nx):
            for cp in dp_out(h, k):
                cp.start()

    def dp_wait(h):
        for k in range(1, nx):
            for cp in dp_out(h, k):
                cp.wait_recv()

    def unpack_gu(h):
        @pl.loop(0, db)
        def _(a):
            for jl in range(own):
                s = idx[nt + jl * db + a]
                wd[a, :, pl.ds((1 + h) * fown + jl * bs, bs)] = wr_gu[h][s]

    a2a_all(*gu_out(0)).wait_recv()
    unpack_gu(0)
    partials_gu(0)

    a2a_all(*dn_out).wait_recv()

    @pl.loop(0, db)
    def _(a):
        for jl in range(own):
            s = idx[stride + nt + jl * db + a]
            wd[a, :, pl.ds(jl * bs, bs)] = wr_dn[s]

    partials(0, 1, store_hg)
    dp_send(0)

    def activations(h):
        @pl.loop(0, own)
        def _(j):
            def total(read, peer):
                acc = read().astype(F32)
                for k in range(1, nx):
                    acc += peer(k).astype(F32)
                return acc

            def gu_total(lo):
                r = pl.ds(pl.multiple_of(j * bs + lo, hb), hb)
                return total(lambda: part[h, r, my_tok], lambda k: psum_in[k, h, r, :])

            gate = gu_total(0)
            up = gu_total(hb)
            hg = total(lambda: part_d[j, h, :, my_tok], lambda k: psum_d[k, j, h])
            sig = 1.0 / (1.0 + jnp.exp(-gate))
            act = gate * sig
            hid_d[j, h, :, my_tok] = (act * up).astype(BF)
            g0 = pl.multiple_of(j * bs, bs)
            hid_g[h, pl.ds(g0, hb), my_tok] = (
                hg * up * sig * (1.0 + gate * (1.0 - sig))
            ).astype(BF)
            hid_g[h, pl.ds(g0 + hb, hb), my_tok] = (hg * act).astype(BF)

    def h_copies(h, k, src):
        tok_src = pl.ds(pl.multiple_of(src * tk, tk), tk)
        dd = lax.rem(d + k, nx)
        return (
            rcopy(
                hid_g.at[h, :, my_tok], hid_g.at[h, :, tok_src], hg_s.at[h, k], hg_r.at[h, k], dd, t
            ),
            rcopy(
                hid_d.at[:, h, :, my_tok],
                hid_d.at[:, h, :, tok_src],
                hd_s.at[h, k],
                hd_r.at[h, k],
                dd,
                t,
            ),
        )

    def h_send(h):
        for k in range(1, nx):
            for cp in h_copies(h, k, d):
                cp.start()

    def h_wait(h):
        for k in range(1, nx):
            for cp in h_copies(h, k, lax.rem(d - k + nx, nx)):
                cp.wait_recv()

    dp_wait(0)
    activations(0)
    h_send(0)

    a2a_all(*gu_out(1)).wait_recv()
    unpack_gu(1)
    partials_gu(1)
    dp_send(1)

    mt = 256 // rr

    def grads(arr, rhs, store):
        @pl.loop(0, db // mt)
        def _(i):
            lhs = xall[arr, pl.ds(i * mt, mt)].reshape(mt * rr, tok)
            res = lax.dot_general(lhs, rhs(), nt_dims, preferred_element_type=F32).astype(BF)
            for jl in range(own):
                store(jl * db + i * mt, res[:, jl * bs : (jl + 1) * bs].reshape(mt, rr, bs))

    def grads_gu(h):
        def store(c0, v):
            gc[h, pl.ds(c0, mt)] = v

        grads(0, lambda: hid_g[h], store)

        @pl.loop(0, nt)
        def _(s):
            gs_gu[h, s] = gc[h, idx[nt + cells + s]]

        gr_gu[h, t] = gs_gu[h, t]

    def gu_back(h):
        return gs_gu.at[h], gr_gu.at[h], ggu_s.at[h], ggu_r.at[h]

    dn_back = (gs_dn, gr_dn, gdn_s, gdn_r)

    h_wait(0)
    grads_gu(0)
    a2a(*gu_back(0), 1, nt)

    dp_wait(1)
    activations(1)
    h_send(1)

    h_wait(1)

    @pl.loop(0, db // mt)
    def _(i):
        arows = pl.ds(i * mt, mt)
        lhs = wd[arows, :, pl.ds(0, fown)].reshape(mt * rr, fown)
        res = jnp.dot(lhs, hid_d[...].reshape(fown, tok), preferred_element_type=F32)
        oall[0, arows] = res.astype(BF).reshape(mt, rr, tok)
        lhs = wd[arows, :, pl.ds(fown, 2 * fown)].reshape(mt * rr, 2 * fown)
        res = jnp.dot(lhs, hid_g[...].reshape(2 * fown, tok), preferred_element_type=F32)
        oall[1, arows] = res.astype(BF).reshape(mt, rr, tok)

    core_out = rcopy(oall.at[1 - c], c_in, co_s, co_r, d, other)
    core_out.start()

    def store_dn(c0, v):
        gd[pl.ds(c0, mt)] = v

    grads(1, lambda: hid_d[...].reshape(fown, tok), store_dn)

    @pl.loop(0, nt)
    def _(s):
        gs_dn[s] = gd[idx[stride + nt + cells + s]]

    gr_dn[t] = gs_dn[t]
    a2a(*dn_back, 1, nt)

    core_out.wait_recv()

    @pl.loop(0, npl)
    def _(p):
        tsum[p] = (oall[c, p].astype(F32) + c_in[p].astype(F32)).astype(BF)

    def yo(k):
        yy = lax.rem(y + k, ny)
        return rcopy(
            tsum.at[row_of(yy)], y_in.at[k], yo_s.at[k], yo_r.at[k], d, (yy * nz + z) * 2 + c
        )

    for k in range(1, ny):
        yo(k).start()

    grads_gu(1)
    a2a(*gu_back(1), 1, mid)

    for k in range(1, ny):
        yo(k).wait_recv()

    @pl.loop(0, nz)
    def _(p):
        acc = tsum[y * nz + p].astype(F32)
        for k in range(1, ny):
            acc += y_in[k, p].astype(F32)
        usum[p] = acc.astype(BF)

    def zo(k):
        zz = lax.rem(z + k, nz)
        return rcopy(
            usum.at[zz], z_in.at[k], zo_s.at[k], zo_r.at[k], d, (y * nz + zz) * 2 + c
        )

    for k in range(1, nz):
        zo(k).start()
    a2a(*gu_back(1), mid, nt)

    a2a_all(*dn_back).wait_recv()
    groups = ne // nx

    @pl.loop(0, groups)
    def _(g):
        for p in range(nx):
            o = idx[stride + nt + cells + nt + g * nx + p]
            zl[g, :, pl.ds(p * bs, bs)] = gr_dn[o]

    for dd in range(nx):
        perm = onehot(
            (nx * bs, bs), lambda r, q: r == (q // rr) * bs + dd * rr + q % rr
        )
        moved = jnp.dot(zl[...].reshape(groups * rr, nx * bs), perm, preferred_element_type=F32)
        zs[dd] = moved.astype(BF).reshape(groups, rr, bs)
    zr[d] = zs[d]

    def zx(k, src):
        dd = lax.rem(d + k, nx)
        return rcopy(zs.at[dd], zr.at[src], zx_s.at[k], zx_r.at[k], dd, t)

    for k in range(1, nx):
        zx(k, d).start()

    for k in range(1, nz):
        zo(k).wait_recv()
    acc = usum[z].astype(F32)
    for k in range(1, nz):
        acc += z_in[k].astype(F32)
    vsum[...] = acc.astype(BF)

    def fo(q):
        return rcopy(
            vsum.at[:, pl.ds(q * tk, tk)],
            f_in.at[c, d % dpc],
            fo_s.at[q],
            fo_r.at[c, d % dpc],
            q,
            chip * 2 + d // dpc,
        )

    def unless_self(q, go):
        @pl.when(jnp.logical_not(jnp.logical_and(q == d, d // dpc == c)))
        def _():
            go(fo(q))

    for q in range(nx):
        unless_self(q, lambda cp: cp.start())

    @pl.when(d // dpc == c)
    def _():
        f_in[c, d % dpc] = vsum[:, my_tok]

    for k in range(1, nx):
        zx(k, lax.rem(d - k + nx, nx)).wait_recv()
    eye_b = onehot((bs, bs), lambda r, q: r == q)

    @pl.loop(0, groups)
    def _(g):
        block = zr[:, g].reshape(nx * rr, bs)
        flip = lax.dot_general(block, eye_b, tn_dims, preferred_element_type=F32)
        dg_ref[pl.ds(g * nx, nx)] = flip.astype(BF).reshape(nx, rr, bs)

    for a in range(2):
        for j in range(dpc):
            src_d = c * dpc + j
            own_piece = jnp.logical_and(src_d == d, a == c)

            @pl.when(jnp.logical_not(own_piece))
            def _():
                rcopy(
                    vsum.at[:, pl.ds(0, tk)],
                    f_in.at[a, j],
                    fo_s.at[0],
                    fo_r.at[a, j],
                    d,
                    other,
                ).wait_recv()

    for a, ref in enumerate((out_ref, in_ref)):
        ref[...] = f_in[a]

    for h in range(2):
        a2a_all(*gu_back(h)).wait_recv()

    @pl.loop(0, ne)
    def _(e):
        o = idx[nt + cells + nt + e]
        for h in range(2):
            stage[e, :, pl.ds(h * bs, bs)] = gr_gu[h, o]

    @pl.loop(0, ne // me_n)
    def _(i):
        es = pl.ds(i * me_n, me_n)
        both = stage[es].reshape(me_n * rr, 2 * bs)
        res = jnp.dot(both, halves, preferred_element_type=F32).astype(BF)
        gg_ref[es] = res[:, :bs].reshape(me_n, rr, bs)
        ug_ref[es] = res[:, bs:].reshape(me_n, rr, bs)

    for a in range(2):
        for j in range(dpc):
            dpx(a, j, lambda cp: cp.wait_send())
    for h in range(2):
        a2a_all(*gu_out(h)).wait_send()
        a2a_all(*gu_back(h)).wait_send()
    a2a_all(*dn_out).wait_send()
    a2a_all(*dn_back).wait_send()
    for k in range(1, nz):
        zg(k).wait_send()
        zo(k).wait_send()
    for k in range(1, ny):
        yg(k).wait_send()
        yo(k).wait_send()
    for k in range(ny):
        to_core(k, c).wait_send()
    for k in range(1, nx):
        for h in range(2):
            for cp in dp_out(h, k) + h_copies(h, k, d):
                cp.wait_send()
        zx(k, d).wait_send()
    core_out.wait_send()
    for q in range(nx):
        unless_self(q, lambda cp: cp.wait_send())


def copy_kernel(n, *refs):
    for i in range(n):
        refs[n + i][...] = refs[i][...]


def per_device(dims, tokens_in, out_grad, gate_blocks, up_blocks, down_blocks, gate_up_index, down_index):
    nx, ny, nz = dims
    nt, ne = gate_up_index.shape[:2]
    npl = ny * nz
    db = npl
    bs = gate_blocks.shape[1]
    tk = tokens_in.shape[0]
    own = FB // nt
    rr = bs // nx
    dpc = nx // 2
    fown = own * bs
    tok = nx * tk
    cells = own * db
    tables = route_tables(
        (
            (gate_up_index[:, :, 1], gate_up_index[:, :, 0]),
            (down_index[:, :, 0], down_index[:, :, 1]),
        ),
        own,
        db,
        lax.axis_index("tensor"),
    )
    v = lambda *s: pltpu.VMEM(s, BF)
    dma = lambda *s: pltpu.SemaphoreType.DMA(s)
    scratch = [
        v(2, ne, rr, bs),
        v(2, ne + 1, rr, bs),
        v(ne, bs, bs),
        v(ne + 1, rr, bs),
        v(2, dpc, rr, tk),
        v(2, nt, rr, bs),
        v(nt + 1, rr, bs),
        v(nt + 1, rr, bs),
        v(nt, rr, bs),
        v(nt + 1, rr, bs),
        v(2, npl, rr, tok),
        v(db, rr, 3 * fown),
        v(2, fown, tok),
        v(nx, 2, fown, tk),
        v(own, 2, bs // 2, tok),
        v(nx, own, 2, bs // 2, tk),
        v(2, fown, tok),
        v(own, 2, bs // 2, tok),
        v(2, npl, rr, tok),
        v(npl, rr, tok),
        v(npl, rr, tok),
        v(ny, nz, rr, tok),
        v(nz, rr, tok),
        v(nz, rr, tok),
        v(rr, tok),
        v(2, dpc, rr, tk),
        v(2, cells, rr, bs),
        v(cells, rr, bs),
        v(2, nt, rr, bs),
        v(2, nt, rr, bs),
        v(nt, rr, bs),
        v(nt, rr, bs),
        v(ne, rr, 2 * bs),
        v(ne // nx, rr, nx * bs),
        v(nx, ne // nx, rr, bs),
        v(nx, ne // nx, rr, bs),
        dma(5),
        dma(2, dpc),
        dma(nx),
        dma(nz),
        dma(nz),
        dma(ny),
        dma(ny),
        dma(ny),
        dma(ny),
        pltpu.SemaphoreType.DMA,
        pltpu.SemaphoreType.DMA,
        dma(2),
        dma(2),
        dma(2, nx),
        dma(2, nx),
        dma(2, nx),
        dma(2, nx),
        dma(2, nx),
        dma(2, nx),
        dma(2, nx),
        dma(2, nx),
        pltpu.SemaphoreType.DMA,
        pltpu.SemaphoreType.DMA,
        dma(ny),
        dma(ny),
        dma(nz),
        dma(nz),
        dma(nx),
        dma(2, dpc),
        pltpu.SemaphoreType.DMA,
        pltpu.SemaphoreType.DMA,
        dma(2),
        dma(2),
        dma(nx),
        dma(nx),
    ]
    vm = pl.BlockSpec(memory_space=pltpu.VMEM)
    hbm = pl.BlockSpec(memory_space=pl.ANY)
    grad = jax.ShapeDtypeStruct((ne, rr, bs), BF)
    act = jax.ShapeDtypeStruct((dpc, rr, tk), BF)
    feat = dpc * rr
    shapes = (act, act, grad, grad, grad)
    results = pl.pallas_call(
        functools.partial(kernel, (nx, ny, nz, ne, own, db)),
        out_shape=shapes,
        in_specs=[pl.BlockSpec(memory_space=pltpu.SMEM)] + [hbm] * 5,
        out_specs=(vm,) * 5,
        scratch_shapes=scratch,
        compiler_params=pltpu.CompilerParams(
            collective_id=0, has_side_effects=True, vmem_limit_bytes=56 * 2**20
        ),
    )(
        tables,
        tokens_in.T.reshape(dpc, rr, tk),
        out_grad.T.reshape(dpc, rr, tk),
        gate_blocks,
        up_blocks,
        down_blocks,
    )
    n = len(shapes)
    results = pl.pallas_call(
        functools.partial(copy_kernel, n),
        out_shape=shapes,
        in_specs=[vm] * n,
        out_specs=(vm,) * n,
    )(*results)
    return tuple(r.reshape(feat, tk).T for r in results[:2]) + tuple(results[2:])


FB = 128
GRID = {4: (4, 8)}


def solution(mesh):
    nx, nt = mesh.shape["dp"], mesh.shape["tensor"]
    ny, nz = GRID[nx]
    in_specs = (
        P("dp", "tensor"),
        P("dp", "tensor"),
        P("tensor", None, None),
        P("tensor", None, None),
        P("tensor", None, None),
        P(),
        P(),
    )
    out_specs = (
        P("dp", "tensor"),
        P("dp", "tensor"),
        P("tensor", "dp", None),
        P("tensor", "dp", None),
        P("tensor", "dp", None),
    )
    return jax.shard_map(
        functools.partial(per_device, (nx, ny, nz)),
        mesh=mesh,
        in_specs=in_specs,
        out_specs=out_specs,
        check_vma=False,
    )
```

```python
import functools

import jax
import jax.numpy as jnp
from jax import lax
from jax.experimental import pallas as pl
from jax.experimental.pallas import tpu as pltpu
from jax.sharding import PartitionSpec as P

MESH = pl.DeviceIdType.MESH
BF = jnp.bfloat16
F32 = jnp.float32


def route_tables(lists, own, width_blocks, me):
    key = jnp.stack([k for k, _ in lists])
    other = jnp.stack([o for _, o in lists])
    nt, ne = key.shape[1:]
    owner = key // own
    cell = (key % own) * width_blocks + other
    my_owner = lax.dynamic_index_in_dim(owner, me, 1, keepdims=False)
    hit = my_owner[:, None, :] == jnp.arange(nt)[None, :, None]
    send = jnp.min(jnp.where(hit, jnp.arange(ne)[None, None, :], ne), axis=2)
    ret = jnp.max(jnp.where(owner == me, cell, -1), axis=2)
    match = ret[:, None, :] == jnp.arange(own * width_blocks)[None, :, None]
    source = jnp.min(jnp.where(match, jnp.arange(nt)[None, None, :], nt), axis=2)
    table = jnp.concatenate([send, source, jnp.maximum(ret, 0), my_owner], axis=1)
    return table.astype(jnp.int32).reshape(-1)


def kernel(
    cfg,
    idx,
    x_hbm,
    dy_hbm,
    gate_hbm,
    up_hbm,
    down_hbm,
    out_ref,
    in_ref,
    gg_ref,
    ug_ref,
    dg_ref,
    gu_in,
    gu_ab,
    dn_in,
    dn_t,
    xs,
    ws_gu,
    wr_a,
    wr_b,
    ws_dn,
    wr_dn,
    xall,
    wd,
    part,
    psum_in,
    part_d,
    psum_d,
    hid_g,
    hid_d,
    oall,
    c_in,
    tsum,
    y_in,
    usum,
    f_in,
    gc,
    gd,
    gs_gu,
    gr_a,
    gr_b,
    gs_dn,
    gr_dn,
    stage,
    zl,
    zs,
    zr,
    load_sem,
    xg_s,
    xg_r,
    yg_s,
    yg_r,
    cg_s,
    cg_r,
    wdn_s,
    wdn_r,
    wgu_s,
    wgu_r,
    ph_s,
    ph_r,
    pd_s,
    pd_r,
    hg_s,
    hg_r,
    hd_s,
    hd_r,
    co_s,
    co_r,
    yo_s,
    yo_r,
    fo_s,
    fo_r,
    gdn_s,
    gdn_r,
    ggu_s,
    ggu_r,
    zx_s,
    zx_r,
):
    nx, ny, nz, ne, own, db = cfg
    wr_gu = (wr_a, wr_b)
    gr_gu = (gr_a, gr_b)
    nt = ny * nz * 2
    npl = ny * nz
    bs = 128
    hb = bs // 2
    tk = 128
    rr = bs // nx
    dpc = nx // 2
    fown = own * bs
    cells = own * db
    stride = nt + cells + nt + ne
    tok = nx * tk
    kall = db * rr
    d = lax.axis_index("dp")
    t = lax.axis_index("tensor")
    c = t % 2
    chip = t // 2
    y = chip // nz
    z = chip % nz
    other = chip * 2 + 1 - c
    my_tok = pl.ds(pl.multiple_of(d * tk, tk), tk)
    nt_dims = (((1,), (1,)), ((), ()))
    tn_dims = (((0,), (0,)), ((), ()))

    def onehot(shape, fn):
        return fn(
            lax.broadcasted_iota(jnp.int32, shape, 0), lax.broadcasted_iota(jnp.int32, shape, 1)
        ).astype(F32).astype(BF)

    def rcopy(src, dst, ssem, rsem, dd, tt):
        return pltpu.make_async_remote_copy(
            src_ref=src,
            dst_ref=dst,
            send_sem=ssem,
            recv_sem=rsem,
            device_id=(dd, tt),
            device_id_type=MESH,
        )

    barrier = pltpu.get_barrier_semaphore()

    rows = pl.ds(pl.multiple_of(d * rr, rr), rr)
    loads = [
        pltpu.make_async_copy(gate_hbm.at[:, rows, :], gu_in.at[0], load_sem.at[0]),
        pltpu.make_async_copy(up_hbm.at[:, rows, :], gu_in.at[1], load_sem.at[1]),
        pltpu.make_async_copy(x_hbm, xs.at[0], load_sem.at[2]),
        pltpu.make_async_copy(dy_hbm, xs.at[1], load_sem.at[3]),
        pltpu.make_async_copy(down_hbm, dn_in, load_sem.at[4]),
    ]
    for cp in loads:
        cp.start()

    @pl.loop(1, nt)
    def _(i):
        pl.semaphore_signal(
            barrier, inc=1, device_id=(d, lax.rem(t + i, nt)), device_id_type=MESH
        )

    for k in range(1, nx):

        @pl.loop(0, 2 * nz)
        def _(i):
            pl.semaphore_signal(
                barrier,
                inc=1,
                device_id=(lax.rem(d + k, nx), y * nz * 2 + i),
                device_id_type=MESH,
            )

    loads[2].wait()
    loads[3].wait()
    pl.semaphore_wait(barrier, nt - 1 + 2 * nz * (nx - 1))

    my_half = pl.ds(pl.multiple_of(c * (tok // 2), tok // 2), tok // 2)
    its_half = pl.ds(pl.multiple_of((1 - c) * (tok // 2), tok // 2), tok // 2)

    def self_piece(plane, zz, core):
        return jnp.logical_and(jnp.logical_and(plane == d, zz == z), core == c)

    def x_out(a, j, zz, go):
        plane = c * dpc + j
        core = d // dpc

        @pl.when(jnp.logical_not(self_piece(plane, zz, core)))
        def _():
            go(
                rcopy(
                    xs.at[a, j],
                    xall.at[a, chip, :, my_tok],
                    xg_s.at[a, j, zz],
                    xg_r.at[a, z, d % dpc],
                    plane,
                    (y * nz + zz) * 2 + core,
                )
            )

    def x_out_all(a, go):
        for k in range(nz):
            for j in range(dpc):
                x_out(a, j, lax.rem(z + k, nz), go)

    def x_wait(a):
        for zz in range(nz):
            for j in range(dpc):
                q = c * dpc + j

                @pl.when(jnp.logical_not(self_piece(q, zz, d // dpc)))
                def _():
                    rcopy(
                        xs.at[0, 0],
                        xall.at[a, y * nz + zz, :, pl.ds(pl.multiple_of(q * tk, tk), tk)],
                        xg_s.at[0, 0, 0],
                        xg_r.at[a, zz, j],
                        d,
                        other,
                    ).wait_recv()

    x_out_all(0, lambda cp: cp.start())

    @pl.when(d // dpc == c)
    def _():
        for a in range(2):
            xall[a, chip, :, my_tok] = xs[a, d % dpc]

    zero_rows = jnp.zeros((rr, bs), BF)
    dn_t[ne] = zero_rows
    wr_dn[nt] = zero_rows
    for h in range(2):
        gu_ab[h, ne] = zero_rows
        wr_gu[h][nt] = zero_rows

    def half_src(i):
        return (i % bs) // hb * bs + i // bs * hb + i % hb

    halves = onehot((2 * bs, 2 * bs), lambda r, q: r == half_src(q))
    loads[0].wait()
    loads[1].wait()
    me_n = 256 // rr

    @pl.loop(0, ne // me_n)
    def _(i):
        es = pl.ds(i * me_n, me_n)
        both = jnp.concatenate(
            [gu_in[0, es].reshape(me_n * rr, bs), gu_in[1, es].reshape(me_n * rr, bs)], axis=1
        )
        res = jnp.dot(both, halves, preferred_element_type=F32).astype(BF)
        for h in range(2):
            gu_ab[h, es] = res[:, h * bs : (h + 1) * bs].reshape(me_n, rr, bs)

    @pl.loop(0, nt)
    def _(s):
        e = idx[s]
        ws_gu[0, s] = gu_ab[0, e]
        ws_gu[1, s] = gu_ab[1, e]

    for h in range(2):
        wr_gu[h][t] = ws_gu[h, t]

    row = 2 * nz

    def a2a_row(src, dst, ssem, rsem):
        @pl.loop(1, row)
        def _(i):
            to = y * row + lax.rem(t % row + i, row)
            rcopy(src.at[to], dst.at[t], ssem, rsem, d, to).start()

    def a2a_off(src, dst, ssem, rsem, lo=0, hi=row):
        @pl.loop(lo, hi)
        def _(i):
            for k in range(1, ny):
                to = lax.rem(y + k, ny) * row + lax.rem(t % row + i, row)
                rcopy(src.at[to], dst.at[t], ssem, rsem, d, to).start()

    def a2a_all(src, dst, ssem, rsem):
        return rcopy(
            src.at[pl.ds(0, nt - 1)], dst.at[pl.ds(0, nt - 1)], ssem, rsem, d, lax.rem(t + 1, nt)
        )

    def gu_out(h):
        return ws_gu.at[h], wr_gu[h], wgu_s.at[h], wgu_r.at[h]

    dn_out = (ws_dn, wr_dn, wdn_s, wdn_r)

    a2a_row(*gu_out(0))
    a2a_off(*gu_out(0))

    loads[4].wait()
    pick = onehot((rr, bs), lambda r, q: q == r + d * rr)
    en = 8 if ne % 8 == 0 else ne

    @pl.loop(0, ne // en)
    def _(i):
        blocks = dn_in[pl.ds(i * en, en)].reshape(en * bs, bs)
        res = lax.dot_general(pick, blocks, nt_dims, preferred_element_type=F32).astype(BF)
        for k in range(en):
            dn_t[i * en + k] = res[:, k * bs : (k + 1) * bs]

    @pl.loop(0, nt)
    def _(s):
        ws_dn[s] = dn_t[idx[stride + s]]

    wr_dn[t] = ws_dn[t]

    def row_of(yy):
        return pl.ds(yy * nz, nz)

    def yg(a, k, src):
        yy = lax.rem(y + k, ny)
        return rcopy(
            xall.at[a, row_of(y), :, my_half],
            xall.at[a, row_of(src), :, my_half],
            yg_s.at[a, k],
            yg_r.at[a, k],
            d,
            (yy * nz + z) * 2 + c,
        )

    def y_send(a):
        for i in range(nz):
            for k in range(1, ny):
                yy = lax.rem(y + k, ny)
                piece = xall.at[a, y * nz + i, :, my_half]
                rcopy(
                    piece, piece, yg_s.at[a, k], yg_r.at[a, k], d, (yy * nz + z) * 2 + c
                ).start()

    def to_core(a, k, lanes):
        yy = lax.rem(y - k + ny, ny)
        return rcopy(
            xall.at[a, row_of(yy), :, my_half],
            xall.at[a, row_of(yy), :, lanes],
            cg_s.at[a, k],
            cg_r.at[a, k],
            d,
            other,
        )

    def y_wait(a):
        for k in range(1, ny):
            yg(a, k, lax.rem(y - k + ny, ny)).wait_recv()
            to_core(a, k, my_half).start()

    def core_wait(a):
        for k in range(ny):
            to_core(a, k, its_half).wait_recv()

    x_wait(0)
    y_send(0)
    to_core(0, 0, my_half).start()
    x_out_all(1, lambda cp: cp.start())
    a2a_row(*gu_out(1))
    a2a_off(*gu_out(1))

    y_wait(0)
    x_wait(1)
    y_send(1)
    to_core(1, 0, my_half).start()
    a2a_row(*dn_out)
    a2a_off(*dn_out)
    core_wait(0)

    def partials(lo, arr, store):
        @pl.loop(0, own)
        def _(f):
            cols = pl.ds(pl.multiple_of(lo + f * bs, bs), bs)
            lhs = wd[:, :, cols].reshape(kall, bs)
            rhs = xall[arr].reshape(kall, tok)
            store(f, lax.dot_general(lhs, rhs, tn_dims, preferred_element_type=F32).astype(BF))

    def partials_gu(h):
        def store(f, res):
            part[h, pl.ds(pl.multiple_of(f * bs, bs), bs), :] = res

        partials((1 + h) * fown, 0, store)

    def store_hg(f, res):
        part_d[f] = res.reshape(2, hb, tok)

    def dp_gu(h, k):
        dd = lax.rem(d + k, nx)
        dst_tok = pl.ds(pl.multiple_of(dd * tk, tk), tk)
        return rcopy(
            part.at[h, :, dst_tok], psum_in.at[k, h], ph_s.at[h, k], ph_r.at[h, k], dd, t
        )

    def dp_dn(k):
        dd = lax.rem(d + k, nx)
        dst_tok = pl.ds(pl.multiple_of(dd * tk, tk), tk)
        return rcopy(part_d.at[:, :, :, dst_tok], psum_d.at[k], pd_s.at[k], pd_r.at[k], dd, t)

    def unpack_gu(h):
        @pl.loop(0, db)
        def _(a):
            for jl in range(own):
                s = idx[nt + jl * db + a]
                wd[a, :, pl.ds((1 + h) * fown + jl * bs, bs)] = wr_gu[h][s]

    for h in range(2):
        a2a_all(*gu_out(h)).wait_recv()
        unpack_gu(h)
        partials_gu(h)
        for k in range(1, nx):
            dp_gu(h, k).start()

    y_wait(1)

    def gu_total(h, j, lo):
        r = pl.ds(pl.multiple_of(j * bs + lo, hb), hb)
        acc = part[h, r, my_tok].astype(F32)
        for k in range(1, nx):
            acc += psum_in[k, h, r, :].astype(F32)
        return acc

    def gate_parts(h, j):
        gate = gu_total(h, j, 0)
        up = gu_total(h, j, hb)
        sig = 1.0 / (1.0 + jnp.exp(-gate))
        return gate, up, sig, gate * sig

    def h_gu(h, k, src):
        tok_src = pl.ds(pl.multiple_of(src * tk, tk), tk)
        dd = lax.rem(d + k, nx)
        return rcopy(
            hid_g.at[h, :, my_tok], hid_g.at[h, :, tok_src], hg_s.at[h, k], hg_r.at[h, k], dd, t
        )

    def h_dn(k, src):
        tok_src = pl.ds(pl.multiple_of(src * tk, tk), tk)
        dd = lax.rem(d + k, nx)
        return rcopy(
            hid_d.at[:, :, :, my_tok], hid_d.at[:, :, :, tok_src], hd_s.at[k], hd_r.at[k], dd, t
        )

    def from_plane(k):
        return lax.rem(d - k + nx, nx)

    for h in range(2):
        for k in range(1, nx):
            dp_gu(h, k).wait_recv()

        @pl.loop(0, own)
        def _(j):
            _, up, _, act = gate_parts(h, j)
            hid_d[j, h, :, my_tok] = (act * up).astype(BF)

    for k in range(1, nx):
        h_dn(k, d).start()

    core_wait(1)
    a2a_all(*dn_out).wait_recv()

    @pl.loop(0, db)
    def _(a):
        for jl in range(own):
            s = idx[stride + nt + jl * db + a]
            wd[a, :, pl.ds(jl * bs, bs)] = wr_dn[s]

    partials(0, 1, store_hg)
    for k in range(1, nx):
        dp_dn(k).start()

    mt = 256 // rr

    def grads(arr, rhs, store):
        @pl.loop(0, db // mt)
        def _(i):
            lhs = xall[arr, pl.ds(i * mt, mt)].reshape(mt * rr, tok)
            res = lax.dot_general(lhs, rhs(), nt_dims, preferred_element_type=F32).astype(BF)
            for jl in range(own):
                store(jl * db + i * mt, res[:, jl * bs : (jl + 1) * bs].reshape(mt, rr, bs))

    def grads_gu(h):
        def store(c0, v):
            gc[h, pl.ds(c0, mt)] = v

        grads(0, lambda: hid_g[h], store)

        @pl.loop(0, nt)
        def _(s):
            gs_gu[h, s] = gc[h, idx[nt + cells + s]]

        gr_gu[h][t] = gs_gu[h, t]

    def gu_back(h):
        return gs_gu.at[h], gr_gu[h], ggu_s.at[h], ggu_r.at[h]

    dn_back = (gs_dn, gr_dn, gdn_s, gdn_r)

    def store_dn(c0, v):
        gd[pl.ds(c0, mt)] = v

    for k in range(1, nx):
        h_dn(k, from_plane(k)).wait_recv()
    grads(1, lambda: hid_d[...].reshape(fown, tok), store_dn)

    @pl.loop(0, nt)
    def _(s):
        gs_dn[s] = gd[idx[stride + nt + cells + s]]

    gr_dn[t] = gs_dn[t]
    a2a_off(*dn_back)
    a2a_row(*dn_back)

    def core_out(a):
        return rcopy(oall.at[a, :, :, its_half], c_in.at[a], co_s.at[a], co_r.at[a], d, other)

    def in_half(a, p):
        return oall[a, p, :, my_half].astype(F32)

    def yo(a, k):
        yy = lax.rem(y + k, ny)
        return rcopy(
            tsum.at[a, row_of(yy)],
            y_in.at[a, k],
            yo_s.at[a, k],
            yo_r.at[a, k],
            d,
            (yy * nz + z) * 2 + c,
        )

    def sum_core(a):
        core_out(a).wait_recv()

        @pl.loop(0, npl)
        def _(p):
            tsum[a, p] = (in_half(a, p) + c_in[a, p].astype(F32)).astype(BF)

        for i in range(nz):
            for k in range(1, ny):
                yy = lax.rem(y + k, ny)
                rcopy(
                    tsum.at[a, yy * nz + i],
                    y_in.at[a, k, i],
                    yo_s.at[a, k],
                    yo_r.at[a, k],
                    d,
                    (yy * nz + z) * 2 + c,
                ).start()

    def fo(a, j, zz, go):
        core = d // dpc
        plane = c * dpc + j

        @pl.when(jnp.logical_not(self_piece(plane, zz, core)))
        def _():
            go(
                rcopy(
                    usum.at[a, zz, :, pl.ds(j * tk, tk)],
                    f_in.at[a, d % dpc, z],
                    fo_s.at[a, j, zz],
                    fo_r.at[a, d % dpc, z],
                    plane,
                    (y * nz + zz) * 2 + core,
                )
            )

    def fo_all(a, go):
        for k in range(nz):
            for j in range(dpc):
                fo(a, j, lax.rem(z + k, nz), go)

    def sum_y(a):
        for k in range(1, ny):
            yo(a, k).wait_recv()

        @pl.loop(0, nz)
        def _(p):
            acc = tsum[a, y * nz + p].astype(F32)
            for k in range(1, ny):
                acc += y_in[a, k, p].astype(F32)
            usum[a, p] = acc.astype(BF)

        fo_all(a, lambda cp: cp.start())

        @pl.when(d // dpc == c)
        def _():
            mine = pl.ds(pl.multiple_of(d % dpc * tk, tk), tk)
            f_in[a, d % dpc, z] = usum[a, z, :, mine]

    def sum_z(a, ref):
        for j in range(dpc):
            for zz in range(nz):

                @pl.when(jnp.logical_not(self_piece(c * dpc + j, zz, d // dpc)))
                def _():
                    rcopy(
                        xs.at[0, 0],
                        f_in.at[a, j, zz],
                        fo_s.at[0, 0, 0],
                        fo_r.at[a, j, zz],
                        d,
                        other,
                    ).wait_recv()

            acc = f_in[a, j, 0].astype(F32)
            for zz in range(1, nz):
                acc += f_in[a, j, zz].astype(F32)
            ref[j] = acc.astype(BF)

    def weights_times(a, lo, size, rhs):
        @pl.loop(0, db // mt)
        def _(i):
            arows = pl.ds(i * mt, mt)
            lhs = wd[arows, :, pl.ds(lo, size)].reshape(mt * rr, size)
            res = jnp.dot(lhs, rhs(), preferred_element_type=F32)
            oall[a, arows] = res.astype(BF).reshape(mt, rr, tok)

    weights_times(0, 0, fown, lambda: hid_d[...].reshape(fown, tok))
    core_out(0).start()

    for k in range(1, nx):
        dp_dn(k).wait_recv()
    for h in range(2):

        @pl.loop(0, own)
        def _(j):
            gate, up, sig, act = gate_parts(h, j)
            hg = part_d[j, h, :, my_tok].astype(F32)
            for k in range(1, nx):
                hg += psum_d[k, j, h].astype(F32)
            g0 = pl.multiple_of(j * bs, bs)
            hid_g[h, pl.ds(g0, hb), my_tok] = (
                hg * up * sig * (1.0 + gate * (1.0 - sig))
            ).astype(BF)
            hid_g[h, pl.ds(g0 + hb, hb), my_tok] = (hg * act).astype(BF)

        for k in range(1, nx):
            h_gu(h, k, d).start()

    sum_core(0)

    for h in range(2):
        for k in range(1, nx):
            h_gu(h, k, from_plane(k)).wait_recv()
        grads_gu(h)
        a2a_off(*gu_back(h))
        a2a_row(*gu_back(h))

    weights_times(1, fown, 2 * fown, lambda: hid_g[...].reshape(2 * fown, tok))
    core_out(1).start()

    sum_y(0)

    sum_core(1)

    a2a_all(*dn_back).wait_recv()
    groups = ne // nx

    @pl.loop(0, groups)
    def _(g):
        for p in range(nx):
            o = idx[stride + nt + cells + nt + g * nx + p]
            zl[g, :, pl.ds(p * bs, bs)] = gr_dn[o]

    for dd in range(nx):
        perm = onehot(
            (nx * bs, bs), lambda r, q: r == (q // rr) * bs + dd * rr + q % rr
        )
        moved = jnp.dot(zl[...].reshape(groups * rr, nx * bs), perm, preferred_element_type=F32)
        zs[dd] = moved.astype(BF).reshape(groups, rr, bs)
    zr[d] = zs[d]

    def zx(k, src):
        dd = lax.rem(d + k, nx)
        return rcopy(zs.at[dd], zr.at[src], zx_s.at[k], zx_r.at[k], dd, t)

    for i in range(groups):
        for k in range(1, nx):
            dd = lax.rem(d + k, nx)
            rcopy(zs.at[dd, i], zr.at[d, i], zx_s.at[k], zx_r.at[k], dd, t).start()

    sum_y(1)

    for k in range(1, nx):
        zx(k, from_plane(k)).wait_recv()
    eye_b = onehot((bs, bs), lambda r, q: r == q)

    @pl.loop(0, groups)
    def _(g):
        block = zr[:, g].reshape(nx * rr, bs)
        flip = lax.dot_general(block, eye_b, tn_dims, preferred_element_type=F32)
        dg_ref[pl.ds(g * nx, nx)] = flip.astype(BF).reshape(nx, rr, bs)

    a2a_all(*gu_back(0)).wait_recv()

    def unpack_half(h):
        @pl.loop(0, ne)
        def _(e):
            stage[e, :, pl.ds(h * bs, bs)] = gr_gu[h][idx[nt + cells + nt + e]]

    unpack_half(0)

    sum_z(0, out_ref)
    sum_z(1, in_ref)

    a2a_all(*gu_back(1)).wait_recv()
    unpack_half(1)

    @pl.loop(0, ne // me_n)
    def _(i):
        es = pl.ds(i * me_n, me_n)
        both = stage[es].reshape(me_n * rr, 2 * bs)
        res = jnp.dot(both, halves, preferred_element_type=F32).astype(BF)
        gg_ref[es] = res[:, :bs].reshape(me_n, rr, bs)
        ug_ref[es] = res[:, bs:].reshape(me_n, rr, bs)

    for a in range(2):
        x_out_all(a, lambda cp: cp.wait_send())
        fo_all(a, lambda cp: cp.wait_send())
        core_out(a).wait_send()
        for k in range(1, ny):
            yg(a, k, y).wait_send()
            yo(a, k).wait_send()
        for k in range(ny):
            to_core(a, k, my_half).wait_send()
    for h in range(2):
        a2a_all(*gu_out(h)).wait_send()
        a2a_all(*gu_back(h)).wait_send()
    a2a_all(*dn_out).wait_send()
    a2a_all(*dn_back).wait_send()
    for k in range(1, nx):
        for h in range(2):
            dp_gu(h, k).wait_send()
            h_gu(h, k, d).wait_send()
        dp_dn(k).wait_send()
        h_dn(k, d).wait_send()
        zx(k, d).wait_send()


def copy_kernel(n, *refs):
    for i in range(n):
        refs[n + i][...] = refs[i][...]


def per_device(dims, tokens_in, out_grad, gate_blocks, up_blocks, down_blocks, gate_up_index, down_index):
    nx, ny, nz = dims
    nt, ne = gate_up_index.shape[:2]
    npl = ny * nz
    db = npl
    bs = gate_blocks.shape[1]
    tk = tokens_in.shape[0]
    own = FB // nt
    rr = bs // nx
    dpc = nx // 2
    fown = own * bs
    tok = nx * tk
    cells = own * db
    tables = route_tables(
        (
            (gate_up_index[:, :, 1], gate_up_index[:, :, 0]),
            (down_index[:, :, 0], down_index[:, :, 1]),
        ),
        own,
        db,
        lax.axis_index("tensor"),
    )
    v = lambda *s: pltpu.VMEM(s, BF)
    dma = lambda *s: pltpu.SemaphoreType.DMA(s)
    scratch = [
        v(2, ne, rr, bs),
        v(2, ne + 1, rr, bs),
        v(ne, bs, bs),
        v(ne + 1, rr, bs),
        v(2, dpc, rr, tk),
        v(2, nt, rr, bs),
        v(nt + 1, rr, bs),
        v(nt + 1, rr, bs),
        v(nt, rr, bs),
        v(nt + 1, rr, bs),
        v(2, npl, rr, tok),
        v(db, rr, 3 * fown),
        v(2, fown, tok),
        v(nx, 2, fown, tk),
        v(own, 2, bs // 2, tok),
        v(nx, own, 2, bs // 2, tk),
        v(2, fown, tok),
        v(own, 2, bs // 2, tok),
        v(2, npl, rr, tok),
        v(2, npl, rr, tok // 2),
        v(2, npl, rr, tok // 2),
        v(2, ny, nz, rr, tok // 2),
        v(2, nz, rr, tok // 2),
        v(2, dpc, nz, rr, tk),
        v(2, cells, rr, bs),
        v(cells, rr, bs),
        v(2, nt, rr, bs),
        v(nt, rr, bs),
        v(nt, rr, bs),
        v(nt, rr, bs),
        v(nt, rr, bs),
        v(ne, rr, 2 * bs),
        v(ne // nx, rr, nx * bs),
        v(nx, ne // nx, rr, bs),
        v(nx, ne // nx, rr, bs),
        dma(5),
        dma(2, dpc, nz),
        dma(2, nz, dpc),
        dma(2, ny),
        dma(2, ny),
        dma(2, ny),
        dma(2, ny),
        pltpu.SemaphoreType.DMA,
        pltpu.SemaphoreType.DMA,
        dma(2),
        dma(2),
        dma(2, nx),
        dma(2, nx),
        dma(nx),
        dma(nx),
        dma(2, nx),
        dma(2, nx),
        dma(nx),
        dma(nx),
        dma(2),
        dma(2),
        dma(2, ny),
        dma(2, ny),
        dma(2, dpc, nz),
        dma(2, dpc, nz),
        pltpu.SemaphoreType.DMA,
        pltpu.SemaphoreType.DMA,
        dma(2),
        dma(2),
        dma(nx),
        dma(nx),
    ]
    vm = pl.BlockSpec(memory_space=pltpu.VMEM)
    hbm = pl.BlockSpec(memory_space=pl.ANY)
    grad = jax.ShapeDtypeStruct((ne, rr, bs), BF)
    act = jax.ShapeDtypeStruct((dpc, rr, tk), BF)
    feat = dpc * rr
    shapes = (act, act, grad, grad, grad)
    results = pl.pallas_call(
        functools.partial(kernel, (nx, ny, nz, ne, own, db)),
        out_shape=shapes,
        in_specs=[pl.BlockSpec(memory_space=pltpu.SMEM)] + [hbm] * 5,
        out_specs=(vm,) * 5,
        scratch_shapes=scratch,
        compiler_params=pltpu.CompilerParams(
            collective_id=0, has_side_effects=True, vmem_limit_bytes=56 * 2**20
        ),
    )(
        tables,
        tokens_in.T.reshape(dpc, rr, tk),
        out_grad.T.reshape(dpc, rr, tk),
        gate_blocks,
        up_blocks,
        down_blocks,
    )
    n = len(shapes)
    results = pl.pallas_call(
        functools.partial(copy_kernel, n),
        out_shape=shapes,
        in_specs=[vm] * n,
        out_specs=(vm,) * n,
    )(*results)
    return tuple(r.reshape(feat, tk).T for r in results[:2]) + tuple(results[2:])


FB = 128
GRID = {4: (4, 8)}


def solution(mesh):
    nx, nt = mesh.shape["dp"], mesh.shape["tensor"]
    ny, nz = GRID[nx]
    in_specs = (
        P("dp", "tensor"),
        P("dp", "tensor"),
        P("tensor", None, None),
        P("tensor", None, None),
        P("tensor", None, None),
        P(),
        P(),
    )
    out_specs = (
        P("dp", "tensor"),
        P("dp", "tensor"),
        P("tensor", "dp", None),
        P("tensor", "dp", None),
        P("tensor", "dp", None),
    )
    return jax.shard_map(
        functools.partial(per_device, (nx, ny, nz)),
        mesh=mesh,
        in_specs=in_specs,
        out_specs=out_specs,
        check_vma=False,
    )
```

```python
import functools

import jax
import jax.numpy as jnp
from jax import lax
from jax.experimental import pallas as pl
from jax.experimental.pallas import tpu as pltpu
from jax.sharding import PartitionSpec as P

MESH = pl.DeviceIdType.MESH
BF = jnp.bfloat16
F32 = jnp.float32


def route_tables(lists, own, width_blocks, me):
    key = jnp.stack([k for k, _ in lists])
    other = jnp.stack([o for _, o in lists])
    nt, ne = key.shape[1:]
    owner = key // own
    cell = (key % own) * width_blocks + other
    my_owner = lax.dynamic_index_in_dim(owner, me, 1, keepdims=False)
    hit = my_owner[:, None, :] == jnp.arange(nt)[None, :, None]
    send = jnp.min(jnp.where(hit, jnp.arange(ne)[None, None, :], ne), axis=2)
    ret = jnp.max(jnp.where(owner == me, cell, -1), axis=2)
    match = ret[:, None, :] == jnp.arange(own * width_blocks)[None, :, None]
    source = jnp.min(jnp.where(match, jnp.arange(nt)[None, None, :], nt), axis=2)
    table = jnp.concatenate([send, source, jnp.maximum(ret, 0), my_owner], axis=1)
    return table.astype(jnp.int32).reshape(-1)


def kernel(
    cfg,
    idx,
    x_hbm,
    dy_hbm,
    gate_hbm,
    up_hbm,
    down_hbm,
    out_ref,
    in_ref,
    gg_ref,
    ug_ref,
    dg_ref,
    gu_in,
    dn_in,
    dn_t,
    xs,
    ws_gu,
    wr_a,
    wr_b,
    ws_dn,
    wr_dn,
    xall,
    wd,
    part,
    psum_in,
    part_d,
    psum_d,
    hid_g,
    hid_d,
    oall,
    c_in,
    tsum,
    y_in,
    usum,
    f_in,
    gc,
    gd,
    gs_gu,
    gr_a,
    gr_b,
    gs_dn,
    gr_dn,
    zl,
    zs,
    zr,
    load_sem,
    xg_s,
    xg_r,
    yg_s,
    yg_r,
    cg_s,
    cg_r,
    wdn_s,
    wdn_r,
    wgu_s,
    wgu_r,
    ph_s,
    ph_r,
    pd_s,
    pd_r,
    hg_s,
    hg_r,
    hd_s,
    hd_r,
    co_s,
    co_r,
    yo_s,
    yo_r,
    fo_s,
    fo_r,
    gdn_s,
    gdn_r,
    ggu_s,
    ggu_r,
    zx_s,
    zx_r,
):
    nx, ny, nz, ne, own, db = cfg
    wr_gu = (wr_a, wr_b)
    gr_gu = (gr_a, gr_b)
    nt = ny * nz * 2
    npl = ny * nz
    bs = 128
    hb = bs // 2
    tk = 128
    rr = bs // nx
    dpc = nx // 2
    fown = own * bs
    cells = own * db
    stride = nt + cells + nt + ne
    tok = nx * tk
    kall = db * rr
    d = lax.axis_index("dp")
    t = lax.axis_index("tensor")
    c = t % 2
    chip = t // 2
    y = chip // nz
    z = chip % nz
    other = chip * 2 + 1 - c
    my_tok = pl.ds(pl.multiple_of(d * tk, tk), tk)
    nt_dims = (((1,), (1,)), ((), ()))
    tn_dims = (((0,), (0,)), ((), ()))

    def onehot(shape, fn):
        return fn(
            lax.broadcasted_iota(jnp.int32, shape, 0), lax.broadcasted_iota(jnp.int32, shape, 1)
        ).astype(F32).astype(BF)

    def rcopy(src, dst, ssem, rsem, dd, tt):
        return pltpu.make_async_remote_copy(
            src_ref=src,
            dst_ref=dst,
            send_sem=ssem,
            recv_sem=rsem,
            device_id=(dd, tt),
            device_id_type=MESH,
        )

    barrier = pltpu.get_barrier_semaphore()

    rows = pl.ds(pl.multiple_of(d * rr, rr), rr)
    loads = [
        pltpu.make_async_copy(gate_hbm.at[:, rows, :], gu_in.at[0, pl.ds(0, ne)], load_sem.at[0]),
        pltpu.make_async_copy(up_hbm.at[:, rows, :], gu_in.at[1, pl.ds(0, ne)], load_sem.at[1]),
        pltpu.make_async_copy(x_hbm, xs.at[0], load_sem.at[2]),
        pltpu.make_async_copy(dy_hbm, xs.at[1], load_sem.at[3]),
        pltpu.make_async_copy(down_hbm, dn_in, load_sem.at[4]),
    ]
    for cp in loads:
        cp.start()

    @pl.loop(1, nt)
    def _(i):
        pl.semaphore_signal(
            barrier, inc=1, device_id=(d, lax.rem(t + i, nt)), device_id_type=MESH
        )

    for k in range(1, nx):

        @pl.loop(0, 2 * nz)
        def _(i):
            pl.semaphore_signal(
                barrier,
                inc=1,
                device_id=(lax.rem(d + k, nx), y * nz * 2 + i),
                device_id_type=MESH,
            )

    zero_rows = jnp.zeros((rr, bs), BF)
    dn_t[ne] = zero_rows
    wr_dn[nt] = zero_rows
    for h in range(2):
        gu_in[h, ne] = zero_rows
        wr_gu[h][nt] = zero_rows
    loads[0].wait()
    loads[1].wait()

    @pl.loop(0, nt)
    def _(s):
        e = idx[s]
        ws_gu[0, s] = gu_in[0, e]
        ws_gu[1, s] = gu_in[1, e]

    for h in range(2):
        wr_gu[h][t] = ws_gu[h, t]

    loads[2].wait()
    loads[3].wait()
    pl.semaphore_wait(barrier, nt - 1 + 2 * nz * (nx - 1))

    my_half = pl.ds(pl.multiple_of(c * (tok // 2), tok // 2), tok // 2)
    its_half = pl.ds(pl.multiple_of((1 - c) * (tok // 2), tok // 2), tok // 2)

    def self_piece(plane, zz, core):
        return jnp.logical_and(jnp.logical_and(plane == d, zz == z), core == c)

    def x_out(a, j, zz, go):
        plane = c * dpc + j
        core = d // dpc

        @pl.when(jnp.logical_not(self_piece(plane, zz, core)))
        def _():
            go(
                rcopy(
                    xs.at[a, j],
                    xall.at[a, chip, :, my_tok],
                    xg_s.at[a, j, zz],
                    xg_r.at[a, z, d % dpc],
                    plane,
                    (y * nz + zz) * 2 + core,
                )
            )

    def x_out_all(a, go):
        for k in range(nz):
            for j in range(dpc):
                x_out(a, j, lax.rem(z + k, nz), go)

    def x_wait(a):
        for zz in range(nz):
            for j in range(dpc):
                q = c * dpc + j

                @pl.when(jnp.logical_not(self_piece(q, zz, d // dpc)))
                def _():
                    rcopy(
                        xs.at[0, 0],
                        xall.at[a, y * nz + zz, :, pl.ds(pl.multiple_of(q * tk, tk), tk)],
                        xg_s.at[0, 0, 0],
                        xg_r.at[a, zz, j],
                        d,
                        other,
                    ).wait_recv()

    x_out_all(0, lambda cp: cp.start())

    @pl.when(d // dpc == c)
    def _():
        for a in range(2):
            xall[a, chip, :, my_tok] = xs[a, d % dpc]

    row = 2 * nz

    def a2a_row(src, dst, ssem, rsem):
        @pl.loop(1, row)
        def _(i):
            to = y * row + lax.rem(t % row + i, row)
            rcopy(src.at[to], dst.at[t], ssem, rsem, d, to).start()

    def a2a_off(src, dst, ssem, rsem, lo=0, hi=row):
        @pl.loop(lo, hi)
        def _(i):
            for k in range(1, ny):
                to = lax.rem(y + k, ny) * row + lax.rem(t % row + i, row)
                rcopy(src.at[to], dst.at[t], ssem, rsem, d, to).start()

    def a2a_all(src, dst, ssem, rsem):
        return rcopy(
            src.at[pl.ds(0, nt - 1)], dst.at[pl.ds(0, nt - 1)], ssem, rsem, d, lax.rem(t + 1, nt)
        )

    def gu_out(h):
        return ws_gu.at[h], wr_gu[h], wgu_s.at[h], wgu_r.at[h]

    dn_out = (ws_dn, wr_dn, wdn_s, wdn_r)

    a2a_row(*gu_out(0))
    a2a_off(*gu_out(0))

    loads[4].wait()
    pick = onehot((rr, bs), lambda r, q: q == r + d * rr)
    en = 8 if ne % 8 == 0 else ne

    @pl.loop(0, ne // en)
    def _(i):
        blocks = dn_in[pl.ds(i * en, en)].reshape(en * bs, bs)
        res = lax.dot_general(pick, blocks, nt_dims, preferred_element_type=F32).astype(BF)
        for k in range(en):
            dn_t[i * en + k] = res[:, k * bs : (k + 1) * bs]

    @pl.loop(0, nt)
    def _(s):
        ws_dn[s] = dn_t[idx[stride + s]]

    wr_dn[t] = ws_dn[t]

    def row_of(yy):
        return pl.ds(yy * nz, nz)

    def yg(a, k, src):
        yy = lax.rem(y + k, ny)
        return rcopy(
            xall.at[a, row_of(y), :, my_half],
            xall.at[a, row_of(src), :, my_half],
            yg_s.at[a, k],
            yg_r.at[a, k],
            d,
            (yy * nz + z) * 2 + c,
        )

    def y_send(a):
        for i in range(nz):
            for k in range(1, ny):
                yy = lax.rem(y + k, ny)
                piece = xall.at[a, y * nz + i, :, my_half]
                rcopy(
                    piece, piece, yg_s.at[a, k], yg_r.at[a, k], d, (yy * nz + z) * 2 + c
                ).start()

    def to_core(a, k, lanes):
        yy = lax.rem(y - k + ny, ny)
        return rcopy(
            xall.at[a, row_of(yy), :, my_half],
            xall.at[a, row_of(yy), :, lanes],
            cg_s.at[a, k],
            cg_r.at[a, k],
            d,
            other,
        )

    def y_wait(a):
        for k in range(1, ny):
            yg(a, k, lax.rem(y - k + ny, ny)).wait_recv()
            to_core(a, k, my_half).start()

    def core_wait(a):
        for k in range(ny):
            to_core(a, k, its_half).wait_recv()

    x_wait(0)
    y_send(0)
    to_core(0, 0, my_half).start()
    x_out_all(1, lambda cp: cp.start())
    a2a_row(*gu_out(1))
    a2a_off(*gu_out(1))

    y_wait(0)
    x_wait(1)
    y_send(1)
    to_core(1, 0, my_half).start()
    a2a_row(*dn_out)
    a2a_off(*dn_out)
    core_wait(0)

    def partials(lo, arr, store):
        @pl.loop(0, own)
        def _(f):
            cols = pl.ds(pl.multiple_of(lo + f * bs, bs), bs)
            lhs = wd[:, :, cols].reshape(kall, bs)
            rhs = xall[arr].reshape(kall, tok)
            store(f, lax.dot_general(lhs, rhs, tn_dims, preferred_element_type=F32).astype(BF))

    def partials_gu(h):
        def store(f, res):
            part[h, pl.ds(pl.multiple_of(f * bs, bs), bs), :] = res

        partials((1 + h) * fown, 0, store)

    def store_hg(f, res):
        part_d[pl.ds(pl.multiple_of(f * bs, bs), bs), :] = res

    def dp_gu(h, k):
        dd = lax.rem(d + k, nx)
        dst_tok = pl.ds(pl.multiple_of(dd * tk, tk), tk)
        return rcopy(
            part.at[h, :, dst_tok], psum_in.at[k, h], ph_s.at[h, k], ph_r.at[h, k], dd, t
        )

    def dp_dn(k):
        dd = lax.rem(d + k, nx)
        dst_tok = pl.ds(pl.multiple_of(dd * tk, tk), tk)
        return rcopy(part_d.at[:, dst_tok], psum_d.at[k], pd_s.at[k], pd_r.at[k], dd, t)

    def unpack_gu(h):
        @pl.loop(0, db)
        def _(a):
            for jl in range(own):
                s = idx[nt + jl * db + a]
                wd[a, :, pl.ds((1 + h) * fown + jl * bs, bs)] = wr_gu[h][s]

    for h in range(2):
        a2a_all(*gu_out(h)).wait_recv()
        unpack_gu(h)
        partials_gu(h)
        for k in range(1, nx):
            dp_gu(h, k).start()

    y_wait(1)

    def plane_sum(mine, theirs):
        acc = mine.astype(F32)
        for k in range(1, nx):
            acc += theirs(k).astype(F32)
        return acc

    def gate_parts(r):
        gate, up = (
            plane_sum(part[h, r, my_tok], lambda k, h=h: psum_in[k, h, r, :]) for h in range(2)
        )
        sig = 1.0 / (1.0 + jnp.exp(-gate))
        return gate, up, sig, gate * sig

    def each_rows(fn):
        @pl.loop(0, fown // hb)
        def _(j):
            fn(pl.ds(pl.multiple_of(j * hb, hb), hb))

    def h_gu(h, k, src):
        tok_src = pl.ds(pl.multiple_of(src * tk, tk), tk)
        dd = lax.rem(d + k, nx)
        return rcopy(
            hid_g.at[h, :, my_tok], hid_g.at[h, :, tok_src], hg_s.at[h, k], hg_r.at[h, k], dd, t
        )

    def h_dn(k, src):
        tok_src = pl.ds(pl.multiple_of(src * tk, tk), tk)
        dd = lax.rem(d + k, nx)
        return rcopy(
            hid_d.at[:, my_tok], hid_d.at[:, tok_src], hd_s.at[k], hd_r.at[k], dd, t
        )

    def from_plane(k):
        return lax.rem(d - k + nx, nx)

    for h in range(2):
        for k in range(1, nx):
            dp_gu(h, k).wait_recv()

    def hidden_rows(r):
        _, up, _, act = gate_parts(r)
        hid_d[r, my_tok] = (act * up).astype(BF)

    each_rows(hidden_rows)
    for k in range(1, nx):
        h_dn(k, d).start()

    core_wait(1)
    a2a_all(*dn_out).wait_recv()

    @pl.loop(0, db)
    def _(a):
        for jl in range(own):
            s = idx[stride + nt + jl * db + a]
            wd[a, :, pl.ds(jl * bs, bs)] = wr_dn[s]

    partials(0, 1, store_hg)
    for k in range(1, nx):
        dp_dn(k).start()

    mt = 256 // rr

    def grads(arr, rhs, store):
        @pl.loop(0, db // mt)
        def _(i):
            lhs = xall[arr, pl.ds(i * mt, mt)].reshape(mt * rr, tok)
            res = lax.dot_general(lhs, rhs(), nt_dims, preferred_element_type=F32).astype(BF)
            for jl in range(own):
                store(jl * db + i * mt, res[:, jl * bs : (jl + 1) * bs].reshape(mt, rr, bs))

    def grads_gu(h):
        def store(c0, v):
            gc[h, pl.ds(c0, mt)] = v

        grads(0, lambda: hid_g[h], store)

        @pl.loop(0, nt)
        def _(s):
            gs_gu[h, s] = gc[h, idx[nt + cells + s]]

        gr_gu[h][t] = gs_gu[h, t]

    def gu_back(h):
        return gs_gu.at[h], gr_gu[h], ggu_s.at[h], ggu_r.at[h]

    dn_back = (gs_dn, gr_dn, gdn_s, gdn_r)

    def store_dn(c0, v):
        gd[pl.ds(c0, mt)] = v

    for k in range(1, nx):
        h_dn(k, from_plane(k)).wait_recv()
    grads(1, lambda: hid_d[...], store_dn)

    @pl.loop(0, nt)
    def _(s):
        gs_dn[s] = gd[idx[stride + nt + cells + s]]

    gr_dn[t] = gs_dn[t]
    a2a_off(*dn_back)
    a2a_row(*dn_back)

    def core_out(a):
        return rcopy(oall.at[a, :, :, its_half], c_in.at[a], co_s.at[a], co_r.at[a], d, other)

    def in_half(a, p):
        return oall[a, p, :, my_half].astype(F32)

    def yo(a, k):
        yy = lax.rem(y + k, ny)
        return rcopy(
            tsum.at[a, row_of(yy)],
            y_in.at[a, k],
            yo_s.at[a, k],
            yo_r.at[a, k],
            d,
            (yy * nz + z) * 2 + c,
        )

    def sum_core(a):
        core_out(a).wait_recv()

        @pl.loop(0, npl)
        def _(p):
            tsum[a, p] = (in_half(a, p) + c_in[a, p].astype(F32)).astype(BF)

        for i in range(nz):
            for k in range(1, ny):
                yy = lax.rem(y + k, ny)
                rcopy(
                    tsum.at[a, yy * nz + i],
                    y_in.at[a, k, i],
                    yo_s.at[a, k],
                    yo_r.at[a, k],
                    d,
                    (yy * nz + z) * 2 + c,
                ).start()

    def fo(a, j, zz, go):
        core = d // dpc
        plane = c * dpc + j

        @pl.when(jnp.logical_not(self_piece(plane, zz, core)))
        def _():
            go(
                rcopy(
                    usum.at[a, zz, :, pl.ds(j * tk, tk)],
                    f_in.at[a, d % dpc, z],
                    fo_s.at[a, j, zz],
                    fo_r.at[a, d % dpc, z],
                    plane,
                    (y * nz + zz) * 2 + core,
                )
            )

    def fo_all(a, go):
        for k in range(nz):
            for j in range(dpc):
                fo(a, j, lax.rem(z + k, nz), go)

    def sum_y(a):
        for k in range(1, ny):
            yo(a, k).wait_recv()

        @pl.loop(0, nz)
        def _(p):
            acc = tsum[a, y * nz + p].astype(F32)
            for k in range(1, ny):
                acc += y_in[a, k, p].astype(F32)
            usum[a, p] = acc.astype(BF)

        fo_all(a, lambda cp: cp.start())

        @pl.when(d // dpc == c)
        def _():
            mine = pl.ds(pl.multiple_of(d % dpc * tk, tk), tk)
            f_in[a, d % dpc, z] = usum[a, z, :, mine]

    def sum_z(a, ref):
        for j in range(dpc):
            for zz in range(nz):

                @pl.when(jnp.logical_not(self_piece(c * dpc + j, zz, d // dpc)))
                def _():
                    rcopy(
                        xs.at[0, 0],
                        f_in.at[a, j, zz],
                        fo_s.at[0, 0, 0],
                        fo_r.at[a, j, zz],
                        d,
                        other,
                    ).wait_recv()

            acc = f_in[a, j, 0].astype(F32)
            for zz in range(1, nz):
                acc += f_in[a, j, zz].astype(F32)
            ref[j] = acc.astype(BF)

    def weights_times(a, lo, size, rhs):
        @pl.loop(0, db // mt)
        def _(i):
            arows = pl.ds(i * mt, mt)
            lhs = wd[arows, :, pl.ds(lo, size)].reshape(mt * rr, size)
            res = jnp.dot(lhs, rhs(), preferred_element_type=F32)
            oall[a, arows] = res.astype(BF).reshape(mt, rr, tok)

    weights_times(0, 0, fown, lambda: hid_d[...])
    core_out(0).start()

    for k in range(1, nx):
        dp_dn(k).wait_recv()

    def grad_rows(r):
        gate, up, sig, act = gate_parts(r)
        hg = plane_sum(part_d[r, my_tok], lambda k: psum_d[k, r, :])
        hid_g[0, r, my_tok] = (hg * up * sig * (1.0 + gate * (1.0 - sig))).astype(BF)
        hid_g[1, r, my_tok] = (hg * act).astype(BF)

    each_rows(grad_rows)
    for h in range(2):
        for k in range(1, nx):
            h_gu(h, k, d).start()

    sum_core(0)

    def h_wait(h):
        for k in range(1, nx):
            h_gu(h, k, from_plane(k)).wait_recv()

    h_wait(0)
    grads_gu(0)
    a2a_off(*gu_back(0))
    a2a_row(*gu_back(0))
    h_wait(1)

    weights_times(1, fown, 2 * fown, lambda: hid_g[...].reshape(2 * fown, tok))
    core_out(1).start()
    grads_gu(1)

    sum_core(1)
    a2a_off(*gu_back(1))
    a2a_row(*gu_back(1))

    sum_y(0)

    a2a_all(*dn_back).wait_recv()
    groups = ne // nx

    @pl.loop(0, groups)
    def _(g):
        for p in range(nx):
            o = idx[stride + nt + cells + nt + g * nx + p]
            zl[g, :, pl.ds(p * bs, bs)] = gr_dn[o]

    for dd in range(nx):
        perm = onehot(
            (nx * bs, bs), lambda r, q: r == (q // rr) * bs + dd * rr + q % rr
        )
        moved = jnp.dot(zl[...].reshape(groups * rr, nx * bs), perm, preferred_element_type=F32)
        zs[dd] = moved.astype(BF).reshape(groups, rr, bs)
    zr[d] = zs[d]

    def zx(k, src):
        dd = lax.rem(d + k, nx)
        return rcopy(zs.at[dd], zr.at[src], zx_s.at[k], zx_r.at[k], dd, t)

    for i in range(groups):
        for k in range(1, nx):
            dd = lax.rem(d + k, nx)
            rcopy(zs.at[dd, i], zr.at[d, i], zx_s.at[k], zx_r.at[k], dd, t).start()

    sum_y(1)

    for k in range(1, nx):
        zx(k, from_plane(k)).wait_recv()
    eye_b = onehot((bs, bs), lambda r, q: r == q)

    @pl.loop(0, groups)
    def _(g):
        block = zr[:, g].reshape(nx * rr, bs)
        flip = lax.dot_general(block, eye_b, tn_dims, preferred_element_type=F32)
        dg_ref[pl.ds(g * nx, nx)] = flip.astype(BF).reshape(nx, rr, bs)

    def unpack(h, ref):
        a2a_all(*gu_back(h)).wait_recv()

        @pl.loop(0, ne)
        def _(e):
            ref[e] = gr_gu[h][idx[nt + cells + nt + e]]

    unpack(0, gg_ref)

    sum_z(0, out_ref)
    sum_z(1, in_ref)

    unpack(1, ug_ref)

    for a in range(2):
        x_out_all(a, lambda cp: cp.wait_send())
        fo_all(a, lambda cp: cp.wait_send())
        core_out(a).wait_send()
        for k in range(1, ny):
            yg(a, k, y).wait_send()
            yo(a, k).wait_send()
        for k in range(ny):
            to_core(a, k, my_half).wait_send()
    for h in range(2):
        a2a_all(*gu_out(h)).wait_send()
        a2a_all(*gu_back(h)).wait_send()
    a2a_all(*dn_out).wait_send()
    a2a_all(*dn_back).wait_send()
    for k in range(1, nx):
        for h in range(2):
            dp_gu(h, k).wait_send()
            h_gu(h, k, d).wait_send()
        dp_dn(k).wait_send()
        h_dn(k, d).wait_send()
        zx(k, d).wait_send()


def copy_kernel(n, *refs):
    sem = refs[-1]
    copies = [pltpu.make_async_copy(refs[i], refs[n + i], sem.at[i]) for i in range(n)]
    for cp in copies:
        cp.start()
    for cp in copies:
        cp.wait()


def per_device(dims, tokens_in, out_grad, gate_blocks, up_blocks, down_blocks, gate_up_index, down_index):
    nx, ny, nz = dims
    nt, ne = gate_up_index.shape[:2]
    npl = ny * nz
    db = npl
    bs = gate_blocks.shape[1]
    tk = tokens_in.shape[0]
    own = FB // nt
    rr = bs // nx
    dpc = nx // 2
    fown = own * bs
    tok = nx * tk
    cells = own * db
    tables = route_tables(
        (
            (gate_up_index[:, :, 1], gate_up_index[:, :, 0]),
            (down_index[:, :, 0], down_index[:, :, 1]),
        ),
        own,
        db,
        lax.axis_index("tensor"),
    )
    v = lambda *s: pltpu.VMEM(s, BF)
    dma = lambda *s: pltpu.SemaphoreType.DMA(s)
    scratch = [
        v(2, ne + 1, rr, bs),
        v(ne, bs, bs),
        v(ne + 1, rr, bs),
        v(2, dpc, rr, tk),
        v(2, nt, rr, bs),
        v(nt + 1, rr, bs),
        v(nt + 1, rr, bs),
        v(nt, rr, bs),
        v(nt + 1, rr, bs),
        v(2, npl, rr, tok),
        v(db, rr, 3 * fown),
        v(2, fown, tok),
        v(nx, 2, fown, tk),
        v(fown, tok),
        v(nx, fown, tk),
        v(2, fown, tok),
        v(fown, tok),
        v(2, npl, rr, tok),
        v(2, npl, rr, tok // 2),
        v(2, npl, rr, tok // 2),
        v(2, ny, nz, rr, tok // 2),
        v(2, nz, rr, tok // 2),
        v(2, dpc, nz, rr, tk),
        v(2, cells, rr, bs),
        v(cells, rr, bs),
        v(2, nt, rr, bs),
        v(nt, rr, bs),
        v(nt, rr, bs),
        v(nt, rr, bs),
        v(nt, rr, bs),
        v(ne // nx, rr, nx * bs),
        v(nx, ne // nx, rr, bs),
        v(nx, ne // nx, rr, bs),
        dma(5),
        dma(2, dpc, nz),
        dma(2, nz, dpc),
        dma(2, ny),
        dma(2, ny),
        dma(2, ny),
        dma(2, ny),
        pltpu.SemaphoreType.DMA,
        pltpu.SemaphoreType.DMA,
        dma(2),
        dma(2),
        dma(2, nx),
        dma(2, nx),
        dma(nx),
        dma(nx),
        dma(2, nx),
        dma(2, nx),
        dma(nx),
        dma(nx),
        dma(2),
        dma(2),
        dma(2, ny),
        dma(2, ny),
        dma(2, dpc, nz),
        dma(2, dpc, nz),
        pltpu.SemaphoreType.DMA,
        pltpu.SemaphoreType.DMA,
        dma(2),
        dma(2),
        dma(nx),
        dma(nx),
    ]
    vm = pl.BlockSpec(memory_space=pltpu.VMEM)
    hbm = pl.BlockSpec(memory_space=pl.ANY)
    grad = jax.ShapeDtypeStruct((ne, rr, bs), BF)
    act = jax.ShapeDtypeStruct((dpc, rr, tk), BF)
    feat = dpc * rr
    shapes = (act, act, grad, grad, grad)
    results = pl.pallas_call(
        functools.partial(kernel, (nx, ny, nz, ne, own, db)),
        out_shape=shapes,
        in_specs=[pl.BlockSpec(memory_space=pltpu.SMEM)] + [hbm] * 5,
        out_specs=(vm,) * 5,
        scratch_shapes=scratch,
        compiler_params=pltpu.CompilerParams(
            collective_id=0, has_side_effects=True, vmem_limit_bytes=56 * 2**20
        ),
    )(
        tables,
        tokens_in.T.reshape(dpc, rr, tk),
        out_grad.T.reshape(dpc, rr, tk),
        gate_blocks,
        up_blocks,
        down_blocks,
    )
    n = len(shapes)
    results = pl.pallas_call(
        functools.partial(copy_kernel, n),
        out_shape=shapes,
        in_specs=[vm] * n,
        out_specs=(hbm,) * n,
        scratch_shapes=[pltpu.SemaphoreType.DMA((n,))],
    )(*results)
    return tuple(r.reshape(feat, tk).T for r in results[:2]) + tuple(results[2:])


FB = 128
GRID = {4: (4, 8)}


def solution(mesh):
    nx, nt = mesh.shape["dp"], mesh.shape["tensor"]
    ny, nz = GRID[nx]
    in_specs = (
        P("dp", "tensor"),
        P("dp", "tensor"),
        P("tensor", None, None),
        P("tensor", None, None),
        P("tensor", None, None),
        P(),
        P(),
    )
    out_specs = (
        P("dp", "tensor"),
        P("dp", "tensor"),
        P("tensor", "dp", None),
        P("tensor", "dp", None),
        P("tensor", "dp", None),
    )
    return jax.shard_map(
        functools.partial(per_device, (nx, ny, nz)),
        mesh=mesh,
        in_specs=in_specs,
        out_specs=out_specs,
        check_vma=False,
    )
```

```python
import functools

import jax
import jax.numpy as jnp
from jax import lax
from jax.experimental import pallas as pl
from jax.experimental.pallas import tpu as pltpu
from jax.sharding import PartitionSpec as P

MESH = pl.DeviceIdType.MESH
BF = jnp.bfloat16
F32 = jnp.float32


def route_tables(lists, own, width_blocks, me):
    key = jnp.stack([k for k, _ in lists])
    other = jnp.stack([o for _, o in lists])
    nt, ne = key.shape[1:]
    owner = key // own
    cell = (key % own) * width_blocks + other
    my_owner = lax.dynamic_index_in_dim(owner, me, 1, keepdims=False)
    hit = my_owner[:, None, :] == jnp.arange(nt)[None, :, None]
    send = jnp.min(jnp.where(hit, jnp.arange(ne)[None, None, :], ne), axis=2)
    ret = jnp.max(jnp.where(owner == me, cell, -1), axis=2)
    match = ret[:, None, :] == jnp.arange(own * width_blocks)[None, :, None]
    source = jnp.min(jnp.where(match, jnp.arange(nt)[None, None, :], nt), axis=2)
    table = jnp.concatenate([send, source, jnp.maximum(ret, 0), my_owner], axis=1)
    return table.astype(jnp.int32).reshape(-1)


def kernel(
    cfg,
    idx,
    x_hbm,
    dy_hbm,
    gate_hbm,
    up_hbm,
    down_hbm,
    out_ref,
    in_ref,
    gg_ref,
    ug_ref,
    dg_ref,
    gu_in,
    dn_in,
    dn_t,
    xs,
    ws_gu,
    wr_a,
    wr_b,
    ws_dn,
    wr_dn,
    xall,
    wd,
    part,
    psum_in,
    part_d,
    psum_d,
    hid_g,
    hid_d,
    oall,
    c_in,
    tsum,
    y_in,
    usum,
    f_in,
    gc,
    gd,
    gs_gu,
    gr_a,
    gr_b,
    gs_dn,
    gr_dn,
    zl,
    zs,
    zr,
    load_sem,
    xg_s,
    xg_r,
    yg_s,
    yg_r,
    cg_s,
    cg_r,
    wdn_s,
    wdn_r,
    wgu_s,
    wgu_r,
    ph_s,
    ph_r,
    pd_s,
    pd_r,
    hg_s,
    hg_r,
    hd_s,
    hd_r,
    co_s,
    co_r,
    yo_s,
    yo_r,
    fo_s,
    fo_r,
    gdn_s,
    gdn_r,
    ggu_s,
    ggu_r,
    zx_s,
    zx_r,
):
    nx, ny, nz, ne, own, db = cfg
    wr_gu = (wr_a, wr_b)
    gr_gu = (gr_a, gr_b)
    nt = ny * nz * 2
    npl = ny * nz
    bs = 128
    hb = bs // 2
    tk = 128
    rr = bs // nx
    dpc = nx // 2
    fown = own * bs
    cells = own * db
    stride = nt + cells + nt + ne
    tok = nx * tk
    kall = db * rr
    d = lax.axis_index("dp")
    t = lax.axis_index("tensor")
    c = t % 2
    chip = t // 2
    y = chip // nz
    z = chip % nz
    other = chip * 2 + 1 - c
    my_tok = pl.ds(pl.multiple_of(d * tk, tk), tk)
    nt_dims = (((1,), (1,)), ((), ()))
    tn_dims = (((0,), (0,)), ((), ()))

    def onehot(shape, fn):
        return fn(
            lax.broadcasted_iota(jnp.int32, shape, 0), lax.broadcasted_iota(jnp.int32, shape, 1)
        ).astype(F32).astype(BF)

    def rcopy(src, dst, ssem, rsem, dd, tt):
        return pltpu.make_async_remote_copy(
            src_ref=src,
            dst_ref=dst,
            send_sem=ssem,
            recv_sem=rsem,
            device_id=(dd, tt),
            device_id_type=MESH,
        )

    barrier = pltpu.get_barrier_semaphore()

    rows = pl.ds(pl.multiple_of(d * rr, rr), rr)
    loads = [
        pltpu.make_async_copy(gate_hbm.at[:, rows, :], gu_in.at[0, pl.ds(0, ne)], load_sem.at[0]),
        pltpu.make_async_copy(up_hbm.at[:, rows, :], gu_in.at[1, pl.ds(0, ne)], load_sem.at[1]),
        pltpu.make_async_copy(x_hbm, xs.at[0], load_sem.at[2]),
        pltpu.make_async_copy(dy_hbm, xs.at[1], load_sem.at[3]),
        pltpu.make_async_copy(down_hbm, dn_in, load_sem.at[4]),
    ]
    for cp in loads:
        cp.start()

    @pl.loop(0, 2 * nz)
    def _(i):
        for k in range(1, nx):
            pl.semaphore_signal(
                barrier,
                inc=1,
                device_id=(lax.rem(d + k, nx), y * nz * 2 + i),
                device_id_type=MESH,
            )
        for k in range(1, ny):
            pl.semaphore_signal(
                barrier,
                inc=1,
                device_id=(d, lax.rem(y + k, ny) * nz * 2 + i),
                device_id_type=MESH,
            )

    @pl.loop(1, 2 * nz)
    def _(i):
        pl.semaphore_signal(
            barrier,
            inc=1,
            device_id=(d, y * nz * 2 + lax.rem(t % (2 * nz) + i, 2 * nz)),
            device_id_type=MESH,
        )

    zero_rows = jnp.zeros((rr, bs), BF)
    dn_t[ne] = zero_rows
    wr_dn[nt] = zero_rows
    for h in range(2):
        gu_in[h, ne] = zero_rows
        wr_gu[h][nt] = zero_rows
    loads[0].wait()
    loads[1].wait()

    @pl.loop(0, nt)
    def _(s):
        e = idx[s]
        ws_gu[0, s] = gu_in[0, e]
        ws_gu[1, s] = gu_in[1, e]

    for h in range(2):
        wr_gu[h][t] = ws_gu[h, t]

    loads[2].wait()
    loads[3].wait()
    pl.semaphore_wait(barrier, nt - 1 + 2 * nz * (nx - 1))

    my_half = pl.ds(pl.multiple_of(c * (tok // 2), tok // 2), tok // 2)
    its_half = pl.ds(pl.multiple_of((1 - c) * (tok // 2), tok // 2), tok // 2)

    def self_piece(plane, zz, core):
        return jnp.logical_and(jnp.logical_and(plane == d, zz == z), core == c)

    def x_out(a, j, zz, go):
        plane = c * dpc + j
        core = d // dpc

        @pl.when(jnp.logical_not(self_piece(plane, zz, core)))
        def _():
            go(
                rcopy(
                    xs.at[a, j],
                    xall.at[a, chip, :, my_tok],
                    xg_s.at[a, j, zz],
                    xg_r.at[a, z, d % dpc],
                    plane,
                    (y * nz + zz) * 2 + core,
                )
            )

    def x_out_all(a, go):
        for k in range(nz):
            for j in range(dpc):
                x_out(a, j, lax.rem(z + k, nz), go)

    def x_wait(a):
        for zz in range(nz):
            for j in range(dpc):
                q = c * dpc + j

                @pl.when(jnp.logical_not(self_piece(q, zz, d // dpc)))
                def _():
                    rcopy(
                        xs.at[0, 0],
                        xall.at[a, y * nz + zz, :, pl.ds(pl.multiple_of(q * tk, tk), tk)],
                        xg_s.at[0, 0, 0],
                        xg_r.at[a, zz, j],
                        d,
                        other,
                    ).wait_recv()

    x_out_all(0, lambda cp: cp.start())

    @pl.when(d // dpc == c)
    def _():
        for a in range(2):
            xall[a, chip, :, my_tok] = xs[a, d % dpc]

    row = 2 * nz

    def a2a_row(src, dst, ssem, rsem):
        @pl.loop(1, row)
        def _(i):
            to = y * row + lax.rem(t % row + i, row)
            rcopy(src.at[to], dst.at[t], ssem, rsem, d, to).start()

    def a2a_off(src, dst, ssem, rsem, lo=0, hi=row):
        @pl.loop(lo, hi)
        def _(i):
            for k in range(1, ny):
                to = lax.rem(y + k, ny) * row + lax.rem(t % row + i, row)
                rcopy(src.at[to], dst.at[t], ssem, rsem, d, to).start()

    def a2a_all(src, dst, ssem, rsem):
        return rcopy(
            src.at[pl.ds(0, nt - 1)], dst.at[pl.ds(0, nt - 1)], ssem, rsem, d, lax.rem(t + 1, nt)
        )

    def gu_out(h):
        return ws_gu.at[h], wr_gu[h], wgu_s.at[h], wgu_r.at[h]

    dn_out = (ws_dn, wr_dn, wdn_s, wdn_r)

    a2a_off(*gu_out(0))
    a2a_row(*gu_out(0))

    loads[4].wait()
    pick = onehot((rr, bs), lambda r, q: q == r + d * rr)
    en = 8 if ne % 8 == 0 else ne

    @pl.loop(0, ne // en)
    def _(i):
        blocks = dn_in[pl.ds(i * en, en)].reshape(en * bs, bs)
        res = lax.dot_general(pick, blocks, nt_dims, preferred_element_type=F32).astype(BF)
        for k in range(en):
            dn_t[i * en + k] = res[:, k * bs : (k + 1) * bs]

    @pl.loop(0, nt)
    def _(s):
        ws_dn[s] = dn_t[idx[stride + s]]

    wr_dn[t] = ws_dn[t]

    def row_of(yy):
        return pl.ds(yy * nz, nz)

    def yg(a, k, src):
        yy = lax.rem(y + k, ny)
        return rcopy(
            xall.at[a, row_of(y), :, my_half],
            xall.at[a, row_of(src), :, my_half],
            yg_s.at[a, k],
            yg_r.at[a, k],
            d,
            (yy * nz + z) * 2 + c,
        )

    def y_send(a):
        for i in range(nz):
            for k in range(1, ny):
                yy = lax.rem(y + k, ny)
                piece = xall.at[a, y * nz + i, :, my_half]
                rcopy(
                    piece, piece, yg_s.at[a, k], yg_r.at[a, k], d, (yy * nz + z) * 2 + c
                ).start()

    def to_core(a, k, lanes):
        yy = lax.rem(y - k + ny, ny)
        return rcopy(
            xall.at[a, row_of(yy), :, my_half],
            xall.at[a, row_of(yy), :, lanes],
            cg_s.at[a, k],
            cg_r.at[a, k],
            d,
            other,
        )

    def y_wait(a):
        for k in range(1, ny):
            yg(a, k, lax.rem(y - k + ny, ny)).wait_recv()
            to_core(a, k, my_half).start()

    def core_wait(a):
        for k in range(ny):
            to_core(a, k, its_half).wait_recv()

    x_wait(0)
    y_send(0)
    to_core(0, 0, my_half).start()
    x_out_all(1, lambda cp: cp.start())
    a2a_off(*gu_out(1))
    a2a_row(*gu_out(1))

    y_wait(0)
    x_wait(1)
    y_send(1)
    to_core(1, 0, my_half).start()
    a2a_row(*dn_out)
    a2a_off(*dn_out)
    core_wait(0)

    def partials(lo, arr, store):
        @pl.loop(0, own)
        def _(f):
            cols = pl.ds(pl.multiple_of(lo + f * bs, bs), bs)
            lhs = wd[:, :, cols].reshape(kall, bs)
            rhs = xall[arr].reshape(kall, tok)
            store(f, lax.dot_general(lhs, rhs, tn_dims, preferred_element_type=F32).astype(BF))

    def partials_gu(h):
        def store(f, res):
            part[h, pl.ds(pl.multiple_of(f * bs, bs), bs), :] = res

        partials((1 + h) * fown, 0, store)

    def store_hg(f, res):
        part_d[pl.ds(pl.multiple_of(f * bs, bs), bs), :] = res

    def dp_gu(h, k):
        dd = lax.rem(d + k, nx)
        dst_tok = pl.ds(pl.multiple_of(dd * tk, tk), tk)
        return rcopy(
            part.at[h, :, dst_tok], psum_in.at[k, h], ph_s.at[h, k], ph_r.at[h, k], dd, t
        )

    def dp_dn(k):
        dd = lax.rem(d + k, nx)
        dst_tok = pl.ds(pl.multiple_of(dd * tk, tk), tk)
        return rcopy(part_d.at[:, dst_tok], psum_d.at[k], pd_s.at[k], pd_r.at[k], dd, t)

    def unpack_gu(h):
        @pl.loop(0, db)
        def _(a):
            for jl in range(own):
                s = idx[nt + jl * db + a]
                wd[a, :, pl.ds((1 + h) * fown + jl * bs, bs)] = wr_gu[h][s]

    for h in range(2):
        a2a_all(*gu_out(h)).wait_recv()
        unpack_gu(h)
        partials_gu(h)
        for k in range(1, nx):
            dp_gu(h, k).start()

    y_wait(1)

    def plane_sum(mine, theirs):
        acc = mine.astype(F32)
        for k in range(1, nx):
            acc += theirs(k).astype(F32)
        return acc

    def gate_parts(r):
        gate, up = (
            plane_sum(part[h, r, my_tok], lambda k, h=h: psum_in[k, h, r, :]) for h in range(2)
        )
        sig = 1.0 / (1.0 + jnp.exp(-gate))
        return gate, up, sig, gate * sig

    def each_rows(fn):
        @pl.loop(0, fown // hb)
        def _(j):
            fn(pl.ds(pl.multiple_of(j * hb, hb), hb))

    def h_gu(h, k, src):
        tok_src = pl.ds(pl.multiple_of(src * tk, tk), tk)
        dd = lax.rem(d + k, nx)
        return rcopy(
            hid_g.at[h, :, my_tok], hid_g.at[h, :, tok_src], hg_s.at[h, k], hg_r.at[h, k], dd, t
        )

    def h_dn(k, src):
        tok_src = pl.ds(pl.multiple_of(src * tk, tk), tk)
        dd = lax.rem(d + k, nx)
        return rcopy(
            hid_d.at[:, my_tok], hid_d.at[:, tok_src], hd_s.at[k], hd_r.at[k], dd, t
        )

    def from_plane(k):
        return lax.rem(d - k + nx, nx)

    for h in range(2):
        for k in range(1, nx):
            dp_gu(h, k).wait_recv()

    def hidden_rows(r):
        _, up, _, act = gate_parts(r)
        hid_d[r, my_tok] = (act * up).astype(BF)

    each_rows(hidden_rows)
    for k in range(1, nx):
        h_dn(k, d).start()

    core_wait(1)
    a2a_all(*dn_out).wait_recv()

    @pl.loop(0, db)
    def _(a):
        for jl in range(own):
            s = idx[stride + nt + jl * db + a]
            wd[a, :, pl.ds(jl * bs, bs)] = wr_dn[s]

    partials(0, 1, store_hg)
    for k in range(1, nx):
        dp_dn(k).start()

    mt = 256 // rr

    def grads(arr, rhs, store):
        @pl.loop(0, db // mt)
        def _(i):
            lhs = xall[arr, pl.ds(i * mt, mt)].reshape(mt * rr, tok)
            res = lax.dot_general(lhs, rhs(), nt_dims, preferred_element_type=F32).astype(BF)
            for jl in range(own):
                store(jl * db + i * mt, res[:, jl * bs : (jl + 1) * bs].reshape(mt, rr, bs))

    def grads_gu(h):
        def store(c0, v):
            gc[h, pl.ds(c0, mt)] = v

        grads(0, lambda: hid_g[h], store)

        @pl.loop(0, nt)
        def _(s):
            gs_gu[h, s] = gc[h, idx[nt + cells + s]]

        gr_gu[h][t] = gs_gu[h, t]

    def gu_back(h):
        return gs_gu.at[h], gr_gu[h], ggu_s.at[h], ggu_r.at[h]

    dn_back = (gs_dn, gr_dn, gdn_s, gdn_r)

    def store_dn(c0, v):
        gd[pl.ds(c0, mt)] = v

    for k in range(1, nx):
        h_dn(k, from_plane(k)).wait_recv()
    grads(1, lambda: hid_d[...], store_dn)

    @pl.loop(0, nt)
    def _(s):
        gs_dn[s] = gd[idx[stride + nt + cells + s]]

    gr_dn[t] = gs_dn[t]
    a2a_off(*dn_back)
    a2a_row(*dn_back)

    def core_out(a):
        return rcopy(oall.at[a, :, :, its_half], c_in.at[a], co_s.at[a], co_r.at[a], d, other)

    def in_half(a, p):
        return oall[a, p, :, my_half].astype(F32)

    def yo(a, k):
        yy = lax.rem(y + k, ny)
        return rcopy(
            tsum.at[a, row_of(yy)],
            y_in.at[a, k],
            yo_s.at[a, k],
            yo_r.at[a, k],
            d,
            (yy * nz + z) * 2 + c,
        )

    def sum_core(a):
        core_out(a).wait_recv()

        @pl.loop(0, npl)
        def _(p):
            tsum[a, p] = (in_half(a, p) + c_in[a, p].astype(F32)).astype(BF)

        for i in range(nz):
            for k in range(1, ny):
                yy = lax.rem(y + k, ny)
                rcopy(
                    tsum.at[a, yy * nz + i],
                    y_in.at[a, k, i],
                    yo_s.at[a, k],
                    yo_r.at[a, k],
                    d,
                    (yy * nz + z) * 2 + c,
                ).start()

    def fo(a, j, zz, go):
        core = d // dpc
        plane = c * dpc + j

        @pl.when(jnp.logical_not(self_piece(plane, zz, core)))
        def _():
            go(
                rcopy(
                    usum.at[a, zz, :, pl.ds(j * tk, tk)],
                    f_in.at[a, d % dpc, z],
                    fo_s.at[a, j, zz],
                    fo_r.at[a, d % dpc, z],
                    plane,
                    (y * nz + zz) * 2 + core,
                )
            )

    def fo_all(a, go):
        for k in range(nz):
            for j in range(dpc):
                fo(a, j, lax.rem(z + k, nz), go)

    def sum_y(a):
        for k in range(1, ny):
            yo(a, k).wait_recv()

        @pl.loop(0, nz)
        def _(p):
            acc = tsum[a, y * nz + p].astype(F32)
            for k in range(1, ny):
                acc += y_in[a, k, p].astype(F32)
            usum[a, p] = acc.astype(BF)

        fo_all(a, lambda cp: cp.start())

        @pl.when(d // dpc == c)
        def _():
            mine = pl.ds(pl.multiple_of(d % dpc * tk, tk), tk)
            f_in[a, d % dpc, z] = usum[a, z, :, mine]

    def sum_z(a, ref):
        for j in range(dpc):
            for zz in range(nz):

                @pl.when(jnp.logical_not(self_piece(c * dpc + j, zz, d // dpc)))
                def _():
                    rcopy(
                        xs.at[0, 0],
                        f_in.at[a, j, zz],
                        fo_s.at[0, 0, 0],
                        fo_r.at[a, j, zz],
                        d,
                        other,
                    ).wait_recv()

            acc = f_in[a, j, 0].astype(F32)
            for zz in range(1, nz):
                acc += f_in[a, j, zz].astype(F32)
            ref[j] = acc.astype(BF)

    def weights_times(a, lo, size, rhs):
        @pl.loop(0, db // mt)
        def _(i):
            arows = pl.ds(i * mt, mt)
            lhs = wd[arows, :, pl.ds(lo, size)].reshape(mt * rr, size)
            res = jnp.dot(lhs, rhs(), preferred_element_type=F32)
            oall[a, arows] = res.astype(BF).reshape(mt, rr, tok)

    weights_times(0, 0, fown, lambda: hid_d[...])
    core_out(0).start()

    for k in range(1, nx):
        dp_dn(k).wait_recv()

    def grad_rows(r):
        gate, up, sig, act = gate_parts(r)
        hg = plane_sum(part_d[r, my_tok], lambda k: psum_d[k, r, :])
        hid_g[0, r, my_tok] = (hg * up * sig * (1.0 + gate * (1.0 - sig))).astype(BF)
        hid_g[1, r, my_tok] = (hg * act).astype(BF)

    each_rows(grad_rows)
    for h in range(2):
        for k in range(1, nx):
            h_gu(h, k, d).start()

    sum_core(0)

    def h_wait(h):
        for k in range(1, nx):
            h_gu(h, k, from_plane(k)).wait_recv()

    h_wait(0)
    grads_gu(0)
    a2a_off(*gu_back(0))
    a2a_row(*gu_back(0))
    h_wait(1)

    weights_times(1, fown, 2 * fown, lambda: hid_g[...].reshape(2 * fown, tok))
    core_out(1).start()
    grads_gu(1)

    sum_core(1)
    a2a_off(*gu_back(1))

    sum_y(0)

    a2a_all(*dn_back).wait_recv()
    groups = ne // nx

    @pl.loop(0, groups)
    def _(g):
        for p in range(nx):
            o = idx[stride + nt + cells + nt + g * nx + p]
            zl[g, :, pl.ds(p * bs, bs)] = gr_dn[o]

    for dd in range(nx):
        perm = onehot(
            (nx * bs, bs), lambda r, q: r == (q // rr) * bs + dd * rr + q % rr
        )
        moved = jnp.dot(zl[...].reshape(groups * rr, nx * bs), perm, preferred_element_type=F32)
        zs[dd] = moved.astype(BF).reshape(groups, rr, bs)
    zr[d] = zs[d]

    def zx(k, src):
        dd = lax.rem(d + k, nx)
        return rcopy(zs.at[dd], zr.at[src], zx_s.at[k], zx_r.at[k], dd, t)

    for i in range(groups):
        for k in range(1, nx):
            dd = lax.rem(d + k, nx)
            rcopy(zs.at[dd, i], zr.at[d, i], zx_s.at[k], zx_r.at[k], dd, t).start()

    sum_y(1)
    a2a_row(*gu_back(1))

    for k in range(1, nx):
        zx(k, from_plane(k)).wait_recv()
    eye_b = onehot((bs, bs), lambda r, q: r == q)

    @pl.loop(0, groups)
    def _(g):
        block = zr[:, g].reshape(nx * rr, bs)
        flip = lax.dot_general(block, eye_b, tn_dims, preferred_element_type=F32)
        dg_ref[pl.ds(g * nx, nx)] = flip.astype(BF).reshape(nx, rr, bs)

    def unpack(h, ref):
        a2a_all(*gu_back(h)).wait_recv()

        @pl.loop(0, ne)
        def _(e):
            ref[e] = gr_gu[h][idx[nt + cells + nt + e]]

    unpack(0, gg_ref)

    sum_z(0, out_ref)
    sum_z(1, in_ref)

    unpack(1, ug_ref)

    for a in range(2):
        x_out_all(a, lambda cp: cp.wait_send())
        fo_all(a, lambda cp: cp.wait_send())
        core_out(a).wait_send()
        for k in range(1, ny):
            yg(a, k, y).wait_send()
            yo(a, k).wait_send()
        for k in range(ny):
            to_core(a, k, my_half).wait_send()
    for h in range(2):
        a2a_all(*gu_out(h)).wait_send()
        a2a_all(*gu_back(h)).wait_send()
    a2a_all(*dn_out).wait_send()
    a2a_all(*dn_back).wait_send()
    for k in range(1, nx):
        for h in range(2):
            dp_gu(h, k).wait_send()
            h_gu(h, k, d).wait_send()
        dp_dn(k).wait_send()
        h_dn(k, d).wait_send()
        zx(k, d).wait_send()


def copy_kernel(n, *refs):
    sem = refs[-1]
    copies = [pltpu.make_async_copy(refs[i], refs[n + i], sem.at[i]) for i in range(n)]
    for cp in copies:
        cp.start()
    for cp in copies:
        cp.wait()


def per_device(dims, tokens_in, out_grad, gate_blocks, up_blocks, down_blocks, gate_up_index, down_index):
    nx, ny, nz = dims
    nt, ne = gate_up_index.shape[:2]
    npl = ny * nz
    db = npl
    bs = gate_blocks.shape[1]
    tk = tokens_in.shape[0]
    own = FB // nt
    rr = bs // nx
    dpc = nx // 2
    fown = own * bs
    tok = nx * tk
    cells = own * db
    tables = route_tables(
        (
            (gate_up_index[:, :, 1], gate_up_index[:, :, 0]),
            (down_index[:, :, 0], down_index[:, :, 1]),
        ),
        own,
        db,
        lax.axis_index("tensor"),
    )
    v = lambda *s: pltpu.VMEM(s, BF)
    dma = lambda *s: pltpu.SemaphoreType.DMA(s)
    scratch = [
        v(2, ne + 1, rr, bs),
        v(ne, bs, bs),
        v(ne + 1, rr, bs),
        v(2, dpc, rr, tk),
        v(2, nt, rr, bs),
        v(nt + 1, rr, bs),
        v(nt + 1, rr, bs),
        v(nt, rr, bs),
        v(nt + 1, rr, bs),
        v(2, npl, rr, tok),
        v(db, rr, 3 * fown),
        v(2, fown, tok),
        v(nx, 2, fown, tk),
        v(fown, tok),
        v(nx, fown, tk),
        v(2, fown, tok),
        v(fown, tok),
        v(2, npl, rr, tok),
        v(2, npl, rr, tok // 2),
        v(2, npl, rr, tok // 2),
        v(2, ny, nz, rr, tok // 2),
        v(2, nz, rr, tok // 2),
        v(2, dpc, nz, rr, tk),
        v(2, cells, rr, bs),
        v(cells, rr, bs),
        v(2, nt, rr, bs),
        v(nt, rr, bs),
        v(nt, rr, bs),
        v(nt, rr, bs),
        v(nt, rr, bs),
        v(ne // nx, rr, nx * bs),
        v(nx, ne // nx, rr, bs),
        v(nx, ne // nx, rr, bs),
        dma(5),
        dma(2, dpc, nz),
        dma(2, nz, dpc),
        dma(2, ny),
        dma(2, ny),
        dma(2, ny),
        dma(2, ny),
        pltpu.SemaphoreType.DMA,
        pltpu.SemaphoreType.DMA,
        dma(2),
        dma(2),
        dma(2, nx),
        dma(2, nx),
        dma(nx),
        dma(nx),
        dma(2, nx),
        dma(2, nx),
        dma(nx),
        dma(nx),
        dma(2),
        dma(2),
        dma(2, ny),
        dma(2, ny),
        dma(2, dpc, nz),
        dma(2, dpc, nz),
        pltpu.SemaphoreType.DMA,
        pltpu.SemaphoreType.DMA,
        dma(2),
        dma(2),
        dma(nx),
        dma(nx),
    ]
    vm = pl.BlockSpec(memory_space=pltpu.VMEM)
    hbm = pl.BlockSpec(memory_space=pl.ANY)
    grad = jax.ShapeDtypeStruct((ne, rr, bs), BF)
    act = jax.ShapeDtypeStruct((dpc, rr, tk), BF)
    feat = dpc * rr
    shapes = (act, act, grad, grad, grad)
    results = pl.pallas_call(
        functools.partial(kernel, (nx, ny, nz, ne, own, db)),
        out_shape=shapes,
        in_specs=[pl.BlockSpec(memory_space=pltpu.SMEM)] + [hbm] * 5,
        out_specs=(vm,) * 5,
        scratch_shapes=scratch,
        compiler_params=pltpu.CompilerParams(
            collective_id=0, has_side_effects=True, vmem_limit_bytes=56 * 2**20
        ),
    )(
        tables,
        tokens_in.T.reshape(dpc, rr, tk),
        out_grad.T.reshape(dpc, rr, tk),
        gate_blocks,
        up_blocks,
        down_blocks,
    )
    n = len(shapes)
    results = pl.pallas_call(
        functools.partial(copy_kernel, n),
        out_shape=shapes,
        in_specs=[vm] * n,
        out_specs=(hbm,) * n,
        scratch_shapes=[pltpu.SemaphoreType.DMA((n,))],
    )(*results)
    return tuple(r.reshape(feat, tk).T for r in results[:2]) + tuple(results[2:])


FB = 128
GRID = {4: (4, 8)}


def solution(mesh):
    nx, nt = mesh.shape["dp"], mesh.shape["tensor"]
    ny, nz = GRID[nx]
    in_specs = (
        P("dp", "tensor"),
        P("dp", "tensor"),
        P("tensor", None, None),
        P("tensor", None, None),
        P("tensor", None, None),
        P(),
        P(),
    )
    out_specs = (
        P("dp", "tensor"),
        P("dp", "tensor"),
        P("tensor", "dp", None),
        P("tensor", "dp", None),
        P("tensor", "dp", None),
    )
    return jax.shard_map(
        functools.partial(per_device, (nx, ny, nz)),
        mesh=mesh,
        in_specs=in_specs,
        out_specs=out_specs,
        check_vma=False,
    )
```

```python
import functools

import jax
import jax.numpy as jnp
from jax import lax
from jax.experimental import pallas as pl
from jax.experimental.pallas import tpu as pltpu
from jax.sharding import PartitionSpec as P

MESH = pl.DeviceIdType.MESH
BF = jnp.bfloat16
F32 = jnp.float32


def route_tables(lists, own, width_blocks, me):
    key = jnp.stack([k for k, _ in lists])
    other = jnp.stack([o for _, o in lists])
    nt, ne = key.shape[1:]
    owner = key // own
    cell = (key % own) * width_blocks + other
    my_owner = lax.dynamic_index_in_dim(owner, me, 1, keepdims=False)
    hit = my_owner[:, None, :] == jnp.arange(nt)[None, :, None]
    send = jnp.min(jnp.where(hit, jnp.arange(ne)[None, None, :], ne), axis=2)
    ret = jnp.max(jnp.where(owner == me, cell, -1), axis=2)
    match = ret[:, None, :] == jnp.arange(own * width_blocks)[None, :, None]
    source = jnp.min(jnp.where(match, jnp.arange(nt)[None, None, :], nt), axis=2)
    table = jnp.concatenate([send, source, jnp.maximum(ret, 0), my_owner], axis=1)
    return table.astype(jnp.int32).reshape(-1)


def kernel(
    cfg,
    idx,
    x_hbm,
    dy_hbm,
    gate_hbm,
    up_hbm,
    down_hbm,
    out_ref,
    in_ref,
    gg_ref,
    ug_ref,
    dg_ref,
    gu_in,
    dn_in,
    dn_t,
    xs,
    ws_gu,
    wr_a,
    wr_b,
    ws_dn,
    wr_dn,
    xall,
    wd,
    part,
    psum_in,
    part_d,
    psum_d,
    hid_g,
    hid_d,
    oall,
    c_in,
    tsum,
    y_in,
    usum,
    f_in,
    gc,
    gd,
    gs_gu,
    gr_a,
    gr_b,
    gs_dn,
    gr_dn,
    zl,
    zs,
    zr,
    load_sem,
    xg_s,
    xg_r,
    yg_s,
    yg_r,
    cg_s,
    cg_r,
    wdn_s,
    wdn_r,
    wgu_s,
    wgu_r,
    ph_s,
    ph_r,
    pd_s,
    pd_r,
    hg_s,
    hg_r,
    hd_s,
    hd_r,
    co_s,
    co_r,
    yo_s,
    yo_r,
    fo_s,
    fo_r,
    gdn_s,
    gdn_r,
    ggu_s,
    ggu_r,
    zx_s,
    zx_r,
):
    nx, ny, nz, ne, own, db = cfg
    wr_gu = (wr_a, wr_b)
    gr_gu = (gr_a, gr_b)
    nt = ny * nz * 2
    npl = ny * nz
    bs = 128
    hb = bs // 2
    tk = 128
    rr = bs // nx
    dpc = nx // 2
    fown = own * bs
    cells = own * db
    stride = nt + cells + nt + ne
    tok = nx * tk
    kall = db * rr
    d = lax.axis_index("dp")
    t = lax.axis_index("tensor")
    c = t % 2
    chip = t // 2
    y = chip // nz
    z = chip % nz
    other = chip * 2 + 1 - c
    my_tok = pl.ds(pl.multiple_of(d * tk, tk), tk)
    nt_dims = (((1,), (1,)), ((), ()))
    tn_dims = (((0,), (0,)), ((), ()))

    def onehot(shape, fn):
        return fn(
            lax.broadcasted_iota(jnp.int32, shape, 0), lax.broadcasted_iota(jnp.int32, shape, 1)
        ).astype(F32).astype(BF)

    def rcopy(src, dst, ssem, rsem, dd, tt):
        return pltpu.make_async_remote_copy(
            src_ref=src,
            dst_ref=dst,
            send_sem=ssem,
            recv_sem=rsem,
            device_id=(dd, tt),
            device_id_type=MESH,
        )

    barrier = pltpu.get_barrier_semaphore()

    rows = pl.ds(pl.multiple_of(d * rr, rr), rr)
    loads = [
        pltpu.make_async_copy(gate_hbm.at[:, rows, :], gu_in.at[0, pl.ds(0, ne)], load_sem.at[0]),
        pltpu.make_async_copy(up_hbm.at[:, rows, :], gu_in.at[1, pl.ds(0, ne)], load_sem.at[1]),
        pltpu.make_async_copy(x_hbm, xs.at[0], load_sem.at[2]),
        pltpu.make_async_copy(dy_hbm, xs.at[1], load_sem.at[3]),
        pltpu.make_async_copy(down_hbm, dn_in, load_sem.at[4]),
    ]
    for cp in loads:
        cp.start()

    @pl.loop(0, 2 * nz)
    def _(i):
        for k in range(1, nx):
            pl.semaphore_signal(
                barrier,
                inc=1,
                device_id=(lax.rem(d + k, nx), y * nz * 2 + i),
                device_id_type=MESH,
            )
        for k in range(1, ny):
            pl.semaphore_signal(
                barrier,
                inc=1,
                device_id=(d, lax.rem(y + k, ny) * nz * 2 + i),
                device_id_type=MESH,
            )

    @pl.loop(1, 2 * nz)
    def _(i):
        pl.semaphore_signal(
            barrier,
            inc=1,
            device_id=(d, y * nz * 2 + lax.rem(t % (2 * nz) + i, 2 * nz)),
            device_id_type=MESH,
        )

    zero_rows = jnp.zeros((rr, bs), BF)
    dn_t[ne] = zero_rows
    wr_dn[nt] = zero_rows
    for h in range(2):
        gu_in[h, ne] = zero_rows
        wr_gu[h][nt] = zero_rows
    loads[0].wait()
    loads[1].wait()

    @pl.loop(0, nt)
    def _(s):
        e = idx[s]
        ws_gu[0, s] = gu_in[0, e]
        ws_gu[1, s] = gu_in[1, e]

    for h in range(2):
        wr_gu[h][t] = ws_gu[h, t]

    loads[2].wait()
    loads[3].wait()
    pl.semaphore_wait(barrier, nt - 1 + 2 * nz * (nx - 1))

    my_half = pl.ds(pl.multiple_of(c * (tok // 2), tok // 2), tok // 2)
    its_half = pl.ds(pl.multiple_of((1 - c) * (tok // 2), tok // 2), tok // 2)

    def self_piece(plane, zz, core):
        return jnp.logical_and(jnp.logical_and(plane == d, zz == z), core == c)

    def x_out(a, j, zz, go):
        plane = c * dpc + j
        core = d // dpc

        @pl.when(jnp.logical_not(self_piece(plane, zz, core)))
        def _():
            go(
                rcopy(
                    xs.at[a, j],
                    xall.at[a, chip, :, my_tok],
                    xg_s.at[a, j, zz],
                    xg_r.at[a, z, d % dpc],
                    plane,
                    (y * nz + zz) * 2 + core,
                )
            )

    def x_out_all(a, go):
        for k in range(nz):
            for j in range(dpc):
                x_out(a, j, lax.rem(z + k, nz), go)

    def x_wait(a):
        for zz in range(nz):
            for j in range(dpc):
                q = c * dpc + j

                @pl.when(jnp.logical_not(self_piece(q, zz, d // dpc)))
                def _():
                    rcopy(
                        xs.at[0, 0],
                        xall.at[a, y * nz + zz, :, pl.ds(pl.multiple_of(q * tk, tk), tk)],
                        xg_s.at[0, 0, 0],
                        xg_r.at[a, zz, j],
                        d,
                        other,
                    ).wait_recv()

    x_out_all(0, lambda cp: cp.start())

    @pl.when(d // dpc == c)
    def _():
        for a in range(2):
            xall[a, chip, :, my_tok] = xs[a, d % dpc]

    row = 2 * nz

    def a2a_row(src, dst, ssem, rsem):
        @pl.loop(1, row)
        def _(i):
            to = y * row + lax.rem(t % row + i, row)
            rcopy(src.at[to], dst.at[t], ssem, rsem, d, to).start()

    def a2a_off(src, dst, ssem, rsem, lo=0, hi=row):
        @pl.loop(lo, hi)
        def _(i):
            for k in range(1, ny):
                to = lax.rem(y + k, ny) * row + lax.rem(t % row + i, row)
                rcopy(src.at[to], dst.at[t], ssem, rsem, d, to).start()

    def a2a_all(src, dst, ssem, rsem):
        return rcopy(
            src.at[pl.ds(0, nt - 1)], dst.at[pl.ds(0, nt - 1)], ssem, rsem, d, lax.rem(t + 1, nt)
        )

    def gu_out(h):
        return ws_gu.at[h], wr_gu[h], wgu_s.at[h], wgu_r.at[h]

    dn_out = (ws_dn, wr_dn, wdn_s, wdn_r)

    a2a_off(*gu_out(0))
    a2a_row(*gu_out(0))

    loads[4].wait()
    pick = onehot((rr, bs), lambda r, q: q == r + d * rr)
    en = 8 if ne % 8 == 0 else ne

    @pl.loop(0, ne // en)
    def _(i):
        blocks = dn_in[pl.ds(i * en, en)].reshape(en * bs, bs)
        res = lax.dot_general(pick, blocks, nt_dims, preferred_element_type=F32).astype(BF)
        for k in range(en):
            dn_t[i * en + k] = res[:, k * bs : (k + 1) * bs]

    @pl.loop(0, nt)
    def _(s):
        ws_dn[s] = dn_t[idx[stride + s]]

    wr_dn[t] = ws_dn[t]

    def row_of(yy):
        return pl.ds(yy * nz, nz)

    def yg(a, k, src):
        yy = lax.rem(y + k, ny)
        return rcopy(
            xall.at[a, row_of(y), :, my_half],
            xall.at[a, row_of(src), :, my_half],
            yg_s.at[a, k],
            yg_r.at[a, k],
            d,
            (yy * nz + z) * 2 + c,
        )

    def y_send(a):
        for i in range(nz):
            for k in range(1, ny):
                yy = lax.rem(y + k, ny)
                piece = xall.at[a, y * nz + i, :, my_half]
                rcopy(
                    piece, piece, yg_s.at[a, k], yg_r.at[a, k], d, (yy * nz + z) * 2 + c
                ).start()

    def to_core(a, k, lanes):
        yy = lax.rem(y - k + ny, ny)
        return rcopy(
            xall.at[a, row_of(yy), :, my_half],
            xall.at[a, row_of(yy), :, lanes],
            cg_s.at[a, k],
            cg_r.at[a, k],
            d,
            other,
        )

    def y_wait(a):
        for k in range(1, ny):
            yg(a, k, lax.rem(y - k + ny, ny)).wait_recv()
            to_core(a, k, my_half).start()

    def core_wait(a):
        for k in range(ny):
            to_core(a, k, its_half).wait_recv()

    x_wait(0)
    y_send(0)
    to_core(0, 0, my_half).start()
    x_out_all(1, lambda cp: cp.start())
    a2a_off(*gu_out(1))
    a2a_row(*gu_out(1))

    y_wait(0)
    x_wait(1)
    y_send(1)
    to_core(1, 0, my_half).start()
    a2a_off(*dn_out)
    a2a_row(*dn_out)
    core_wait(0)

    def partials(lo, arr, store):
        @pl.loop(0, own)
        def _(f):
            cols = pl.ds(pl.multiple_of(lo + f * bs, bs), bs)
            lhs = wd[:, :, cols].reshape(kall, bs)
            rhs = xall[arr].reshape(kall, tok)
            store(f, lax.dot_general(lhs, rhs, tn_dims, preferred_element_type=F32).astype(BF))

    def partials_gu(h):
        def store(f, res):
            part[h, pl.ds(pl.multiple_of(f * bs, bs), bs), :] = res

        partials((1 + h) * fown, 0, store)

    def store_hg(f, res):
        part_d[pl.ds(pl.multiple_of(f * bs, bs), bs), :] = res

    def dp_gu(h, k):
        dd = lax.rem(d + k, nx)
        dst_tok = pl.ds(pl.multiple_of(dd * tk, tk), tk)
        return rcopy(
            part.at[h, :, dst_tok], psum_in.at[k, h], ph_s.at[h, k], ph_r.at[h, k], dd, t
        )

    def dp_dn(k):
        dd = lax.rem(d + k, nx)
        dst_tok = pl.ds(pl.multiple_of(dd * tk, tk), tk)
        return rcopy(part_d.at[:, dst_tok], psum_d.at[k], pd_s.at[k], pd_r.at[k], dd, t)

    def unpack_gu(h):
        @pl.loop(0, db)
        def _(a):
            for jl in range(own):
                s = idx[nt + jl * db + a]
                wd[a, :, pl.ds((1 + h) * fown + jl * bs, bs)] = wr_gu[h][s]

    for h in range(2):
        a2a_all(*gu_out(h)).wait_recv()
        unpack_gu(h)
        partials_gu(h)
        for k in range(1, nx):
            dp_gu(h, k).start()

    y_wait(1)

    def plane_sum(mine, theirs):
        acc = mine.astype(F32)
        for k in range(1, nx):
            acc += theirs(k).astype(F32)
        return acc

    def gate_parts(r):
        gate, up = (
            plane_sum(part[h, r, my_tok], lambda k, h=h: psum_in[k, h, r, :]) for h in range(2)
        )
        sig = 1.0 / (1.0 + jnp.exp(-gate))
        return gate, up, sig, gate * sig

    def each_rows(fn):
        @pl.loop(0, fown // hb)
        def _(j):
            fn(pl.ds(pl.multiple_of(j * hb, hb), hb))

    def h_gu(h, k, src):
        tok_src = pl.ds(pl.multiple_of(src * tk, tk), tk)
        dd = lax.rem(d + k, nx)
        return rcopy(
            hid_g.at[h, :, my_tok], hid_g.at[h, :, tok_src], hg_s.at[h, k], hg_r.at[h, k], dd, t
        )

    def h_dn(k, src):
        tok_src = pl.ds(pl.multiple_of(src * tk, tk), tk)
        dd = lax.rem(d + k, nx)
        return rcopy(
            hid_d.at[:, my_tok], hid_d.at[:, tok_src], hd_s.at[k], hd_r.at[k], dd, t
        )

    def from_plane(k):
        return lax.rem(d - k + nx, nx)

    for h in range(2):
        for k in range(1, nx):
            dp_gu(h, k).wait_recv()

    def hidden_rows(r):
        _, up, _, act = gate_parts(r)
        hid_d[r, my_tok] = (act * up).astype(BF)

    each_rows(hidden_rows)
    for k in range(1, nx):
        h_dn(k, d).start()

    core_wait(1)
    a2a_all(*dn_out).wait_recv()

    @pl.loop(0, db)
    def _(a):
        for jl in range(own):
            s = idx[stride + nt + jl * db + a]
            wd[a, :, pl.ds(jl * bs, bs)] = wr_dn[s]

    partials(0, 1, store_hg)
    for k in range(1, nx):
        dp_dn(k).start()

    mt = 256 // rr

    def grads(arr, rhs, store):
        @pl.loop(0, db // mt)
        def _(i):
            lhs = xall[arr, pl.ds(i * mt, mt)].reshape(mt * rr, tok)
            res = lax.dot_general(lhs, rhs(), nt_dims, preferred_element_type=F32).astype(BF)
            for jl in range(own):
                store(jl * db + i * mt, res[:, jl * bs : (jl + 1) * bs].reshape(mt, rr, bs))

    def grads_gu(h):
        def store(c0, v):
            gc[h, pl.ds(c0, mt)] = v

        grads(0, lambda: hid_g[h], store)

        @pl.loop(0, nt)
        def _(s):
            gs_gu[h, s] = gc[h, idx[nt + cells + s]]

        gr_gu[h][t] = gs_gu[h, t]

    def gu_back(h):
        return gs_gu.at[h], gr_gu[h], ggu_s.at[h], ggu_r.at[h]

    dn_back = (gs_dn, gr_dn, gdn_s, gdn_r)

    def store_dn(c0, v):
        gd[pl.ds(c0, mt)] = v

    for k in range(1, nx):
        h_dn(k, from_plane(k)).wait_recv()
    grads(1, lambda: hid_d[...], store_dn)

    @pl.loop(0, nt)
    def _(s):
        gs_dn[s] = gd[idx[stride + nt + cells + s]]

    gr_dn[t] = gs_dn[t]
    a2a_off(*dn_back)
    a2a_row(*dn_back)

    def core_out(a):
        return rcopy(oall.at[a, :, :, its_half], c_in.at[a], co_s.at[a], co_r.at[a], d, other)

    def in_half(a, p):
        return oall[a, p, :, my_half].astype(F32)

    def yo(a, k):
        yy = lax.rem(y + k, ny)
        return rcopy(
            tsum.at[a, row_of(yy)],
            y_in.at[a, k],
            yo_s.at[a, k],
            yo_r.at[a, k],
            d,
            (yy * nz + z) * 2 + c,
        )

    def sum_core(a):
        core_out(a).wait_recv()

        @pl.loop(0, npl)
        def _(p):
            tsum[a, p] = (in_half(a, p) + c_in[a, p].astype(F32)).astype(BF)

        for i in range(nz):
            for k in range(1, ny):
                yy = lax.rem(y + k, ny)
                rcopy(
                    tsum.at[a, yy * nz + i],
                    y_in.at[a, k, i],
                    yo_s.at[a, k],
                    yo_r.at[a, k],
                    d,
                    (yy * nz + z) * 2 + c,
                ).start()

    def fo(a, j, zz, go):
        core = d // dpc
        plane = c * dpc + j

        @pl.when(jnp.logical_not(self_piece(plane, zz, core)))
        def _():
            go(
                rcopy(
                    usum.at[a, zz, :, pl.ds(j * tk, tk)],
                    f_in.at[a, d % dpc, z],
                    fo_s.at[a, j, zz],
                    fo_r.at[a, d % dpc, z],
                    plane,
                    (y * nz + zz) * 2 + core,
                )
            )

    def fo_all(a, go):
        for k in range(nz):
            for j in range(dpc):
                fo(a, j, lax.rem(z + k, nz), go)

    def sum_y(a):
        for k in range(1, ny):
            yo(a, k).wait_recv()

        @pl.loop(0, nz)
        def _(p):
            acc = tsum[a, y * nz + p].astype(F32)
            for k in range(1, ny):
                acc += y_in[a, k, p].astype(F32)
            usum[a, p] = acc.astype(BF)

        fo_all(a, lambda cp: cp.start())

        @pl.when(d // dpc == c)
        def _():
            mine = pl.ds(pl.multiple_of(d % dpc * tk, tk), tk)
            f_in[a, d % dpc, z] = usum[a, z, :, mine]

    def sum_z(a, ref):
        for j in range(dpc):
            for zz in range(nz):

                @pl.when(jnp.logical_not(self_piece(c * dpc + j, zz, d // dpc)))
                def _():
                    rcopy(
                        xs.at[0, 0],
                        f_in.at[a, j, zz],
                        fo_s.at[0, 0, 0],
                        fo_r.at[a, j, zz],
                        d,
                        other,
                    ).wait_recv()

            acc = f_in[a, j, 0].astype(F32)
            for zz in range(1, nz):
                acc += f_in[a, j, zz].astype(F32)
            ref[j] = acc.astype(BF)

    def weights_times(a, lo, size, rhs):
        @pl.loop(0, db // mt)
        def _(i):
            arows = pl.ds(i * mt, mt)
            lhs = wd[arows, :, pl.ds(lo, size)].reshape(mt * rr, size)
            res = jnp.dot(lhs, rhs(), preferred_element_type=F32)
            oall[a, arows] = res.astype(BF).reshape(mt, rr, tok)

    weights_times(0, 0, fown, lambda: hid_d[...])
    core_out(0).start()

    for k in range(1, nx):
        dp_dn(k).wait_recv()

    def grad_rows(r):
        gate, up, sig, act = gate_parts(r)
        hg = plane_sum(part_d[r, my_tok], lambda k: psum_d[k, r, :])
        hid_g[0, r, my_tok] = (hg * up * sig * (1.0 + gate * (1.0 - sig))).astype(BF)
        hid_g[1, r, my_tok] = (hg * act).astype(BF)

    each_rows(grad_rows)
    for h in range(2):
        for k in range(1, nx):
            h_gu(h, k, d).start()

    sum_core(0)

    def h_wait(h):
        for k in range(1, nx):
            h_gu(h, k, from_plane(k)).wait_recv()

    h_wait(0)
    grads_gu(0)
    a2a_off(*gu_back(0))
    a2a_row(*gu_back(0))
    h_wait(1)

    weights_times(1, fown, 2 * fown, lambda: hid_g[...].reshape(2 * fown, tok))
    core_out(1).start()
    grads_gu(1)

    sum_core(1)
    a2a_off(*gu_back(1))

    sum_y(0)

    a2a_all(*dn_back).wait_recv()
    groups = ne // nx

    @pl.loop(0, groups)
    def _(g):
        for p in range(nx):
            o = idx[stride + nt + cells + nt + g * nx + p]
            zl[g, :, pl.ds(p * bs, bs)] = gr_dn[o]

    for dd in range(nx):
        perm = onehot(
            (nx * bs, bs), lambda r, q: r == (q // rr) * bs + dd * rr + q % rr
        )
        moved = jnp.dot(zl[...].reshape(groups * rr, nx * bs), perm, preferred_element_type=F32)
        zs[dd] = moved.astype(BF).reshape(groups, rr, bs)
    zr[d] = zs[d]

    def zx(k, src):
        dd = lax.rem(d + k, nx)
        return rcopy(zs.at[dd], zr.at[src], zx_s.at[k], zx_r.at[k], dd, t)

    for i in range(groups):
        for k in range(1, nx):
            dd = lax.rem(d + k, nx)
            rcopy(zs.at[dd, i], zr.at[d, i], zx_s.at[k], zx_r.at[k], dd, t).start()

    sum_y(1)
    a2a_row(*gu_back(1))

    for k in range(1, nx):
        zx(k, from_plane(k)).wait_recv()
    eye_b = onehot((bs, bs), lambda r, q: r == q)

    @pl.loop(0, groups)
    def _(g):
        block = zr[:, g].reshape(nx * rr, bs)
        flip = lax.dot_general(block, eye_b, tn_dims, preferred_element_type=F32)
        dg_ref[pl.ds(g * nx, nx)] = flip.astype(BF).reshape(nx, rr, bs)

    def unpack(h, ref):
        a2a_all(*gu_back(h)).wait_recv()

        @pl.loop(0, ne)
        def _(e):
            ref[e] = gr_gu[h][idx[nt + cells + nt + e]]

    unpack(0, gg_ref)

    sum_z(0, out_ref)
    sum_z(1, in_ref)

    unpack(1, ug_ref)

    for a in range(2):
        x_out_all(a, lambda cp: cp.wait_send())
        fo_all(a, lambda cp: cp.wait_send())
        core_out(a).wait_send()
        for k in range(1, ny):
            yg(a, k, y).wait_send()
            yo(a, k).wait_send()
        for k in range(ny):
            to_core(a, k, my_half).wait_send()
    for h in range(2):
        a2a_all(*gu_out(h)).wait_send()
        a2a_all(*gu_back(h)).wait_send()
    a2a_all(*dn_out).wait_send()
    a2a_all(*dn_back).wait_send()
    for k in range(1, nx):
        for h in range(2):
            dp_gu(h, k).wait_send()
            h_gu(h, k, d).wait_send()
        dp_dn(k).wait_send()
        h_dn(k, d).wait_send()
        zx(k, d).wait_send()


def copy_kernel(n, *refs):
    sem = refs[-1]
    copies = [pltpu.make_async_copy(refs[i], refs[n + i], sem.at[i]) for i in range(n)]
    for cp in copies:
        cp.start()
    for cp in copies:
        cp.wait()


def per_device(dims, tokens_in, out_grad, gate_blocks, up_blocks, down_blocks, gate_up_index, down_index):
    nx, ny, nz = dims
    nt, ne = gate_up_index.shape[:2]
    npl = ny * nz
    db = npl
    bs = gate_blocks.shape[1]
    tk = tokens_in.shape[0]
    own = FB // nt
    rr = bs // nx
    dpc = nx // 2
    fown = own * bs
    tok = nx * tk
    cells = own * db
    tables = route_tables(
        (
            (gate_up_index[:, :, 1], gate_up_index[:, :, 0]),
            (down_index[:, :, 0], down_index[:, :, 1]),
        ),
        own,
        db,
        lax.axis_index("tensor"),
    )
    v = lambda *s: pltpu.VMEM(s, BF)
    dma = lambda *s: pltpu.SemaphoreType.DMA(s)
    scratch = [
        v(2, ne + 1, rr, bs),
        v(ne, bs, bs),
        v(ne + 1, rr, bs),
        v(2, dpc, rr, tk),
        v(2, nt, rr, bs),
        v(nt + 1, rr, bs),
        v(nt + 1, rr, bs),
        v(nt, rr, bs),
        v(nt + 1, rr, bs),
        v(2, npl, rr, tok),
        v(db, rr, 3 * fown),
        v(2, fown, tok),
        v(nx, 2, fown, tk),
        v(fown, tok),
        v(nx, fown, tk),
        v(2, fown, tok),
        v(fown, tok),
        v(2, npl, rr, tok),
        v(2, npl, rr, tok // 2),
        v(2, npl, rr, tok // 2),
        v(2, ny, nz, rr, tok // 2),
        v(2, nz, rr, tok // 2),
        v(2, dpc, nz, rr, tk),
        v(2, cells, rr, bs),
        v(cells, rr, bs),
        v(2, nt, rr, bs),
        v(nt, rr, bs),
        v(nt, rr, bs),
        v(nt, rr, bs),
        v(nt, rr, bs),
        v(ne // nx, rr, nx * bs),
        v(nx, ne // nx, rr, bs),
        v(nx, ne // nx, rr, bs),
        dma(5),
        dma(2, dpc, nz),
        dma(2, nz, dpc),
        dma(2, ny),
        dma(2, ny),
        dma(2, ny),
        dma(2, ny),
        pltpu.SemaphoreType.DMA,
        pltpu.SemaphoreType.DMA,
        dma(2),
        dma(2),
        dma(2, nx),
        dma(2, nx),
        dma(nx),
        dma(nx),
        dma(2, nx),
        dma(2, nx),
        dma(nx),
        dma(nx),
        dma(2),
        dma(2),
        dma(2, ny),
        dma(2, ny),
        dma(2, dpc, nz),
        dma(2, dpc, nz),
        pltpu.SemaphoreType.DMA,
        pltpu.SemaphoreType.DMA,
        dma(2),
        dma(2),
        dma(nx),
        dma(nx),
    ]
    vm = pl.BlockSpec(memory_space=pltpu.VMEM)
    hbm = pl.BlockSpec(memory_space=pl.ANY)
    grad = jax.ShapeDtypeStruct((ne, rr, bs), BF)
    act = jax.ShapeDtypeStruct((dpc, rr, tk), BF)
    feat = dpc * rr
    shapes = (act, act, grad, grad, grad)
    results = pl.pallas_call(
        functools.partial(kernel, (nx, ny, nz, ne, own, db)),
        out_shape=shapes,
        in_specs=[pl.BlockSpec(memory_space=pltpu.SMEM)] + [hbm] * 5,
        out_specs=(vm,) * 5,
        scratch_shapes=scratch,
        compiler_params=pltpu.CompilerParams(
            collective_id=0, has_side_effects=True, vmem_limit_bytes=56 * 2**20
        ),
    )(
        tables,
        tokens_in.T.reshape(dpc, rr, tk),
        out_grad.T.reshape(dpc, rr, tk),
        gate_blocks,
        up_blocks,
        down_blocks,
    )
    n = len(shapes)
    results = pl.pallas_call(
        functools.partial(copy_kernel, n),
        out_shape=shapes,
        in_specs=[vm] * n,
        out_specs=(hbm,) * n,
        scratch_shapes=[pltpu.SemaphoreType.DMA((n,))],
    )(*results)
    return tuple(r.reshape(feat, tk).T for r in results[:2]) + tuple(results[2:])


FB = 128
GRID = {4: (4, 8)}


def solution(mesh):
    nx, nt = mesh.shape["dp"], mesh.shape["tensor"]
    ny, nz = GRID[nx]
    in_specs = (
        P("dp", "tensor"),
        P("dp", "tensor"),
        P("tensor", None, None),
        P("tensor", None, None),
        P("tensor", None, None),
        P(),
        P(),
    )
    out_specs = (
        P("dp", "tensor"),
        P("dp", "tensor"),
        P("tensor", "dp", None),
        P("tensor", "dp", None),
        P("tensor", "dp", None),
    )
    return jax.shard_map(
        functools.partial(per_device, (nx, ny, nz)),
        mesh=mesh,
        in_specs=in_specs,
        out_specs=out_specs,
        check_vma=False,
    )
```
